768 devices in a mesh: fact: 96 (over z, y), key: 8 (over x, core).
Axes of the slice: x: 4, y: 8, z: 12, core: 2. Of those that a mesh axis runs over, the one named last changes fastest.
Arguments:
- fact_features: bfloat16 [786432, 256], P(('fact', 'key')), may hold values from -6 to 6
- targets: bfloat16 [786432, 128], P(('fact', 'key')), may hold values from -6 to 6
- fact_keys: int32 [786432], P(('fact', 'key')), may hold values from 0 to 6143, as said below
- fill_counts: int32 [768, 8], P(('fact', 'key')), may hold values from 32 to 128, as said below
- dim_features: bfloat16 [6144, 1024], P(('fact', 'key')), may hold values from -6 to 6
- fact_weight: bfloat16 [256, 128], replicated, may hold values from -0.375 to 0.375
- dim_weight: bfloat16 [1024, 128], replicated, may hold values from -0.1875 to 0.1875
Outputs:
- grad_fact: float32 [256, 128], replicated
- grad_dim: float32 [1024, 128], replicated
The draws below stay inside these ranges and needn't reach their ends.
Inputs may be any that keep to these rules, and one draw needn't show every extreme that they name: `fact_keys`: the slot at position s lies in bucket b = (s // 128) % 8, and its key g satisfies (g // 8) % 8 = b. `fill_counts`: each device has some bucket with all 128 slots live.
All inputs are finite; a program needn't handle non-finite values.
Results may differ from the reference program's by a relative error of at most 0.0013.
Values may be sent and summed in bfloat16 or wider, within the bound.
No kernel may reach another device: no remote copies, remote signals or barrier semaphores. Data moves between devices by JAX's collectives and lax.ppermute only.
A program may use at most 32 MiB of HBM per device.

```python
import jax
import jax.numpy as jnp
from jax import lax

DS = 256
DR = 1024
OUTS = 128
CAP = 128
KD = 8
DIM_KEYS = 6144
ROWS = 786432
N_FACT = 96
N_KEY = 8


def draw_fact_keys(key, part):
    slot_index = jnp.arange(ROWS, dtype=jnp.int32)
    bucket = slot_index // CAP % N_KEY
    owner_row = jax.random.randint(jax.random.fold_in(key, 11), (ROWS,), 0, N_FACT, dtype=jnp.int32)
    within = jax.random.randint(jax.random.fold_in(key, 12), (ROWS,), 0, KD, dtype=jnp.int32)
    return ((owner_row * N_KEY + bucket) * KD + within).astype(jnp.int32)


def draw_fill_counts(key, part):
    device_rows = N_FACT * N_KEY
    counts_drawn = jax.random.randint(jax.random.fold_in(key, 21), (device_rows, N_KEY), CAP // 4, CAP + 1, dtype=jnp.int32)
    full_bucket = jax.random.randint(jax.random.fold_in(key, 22), (device_rows, 1), 0, N_KEY, dtype=jnp.int32)
    bucket_index = jnp.arange(N_KEY, dtype=jnp.int32)[None, :]
    return jnp.where(bucket_index == full_bucket, jnp.int32(CAP), counts_drawn).astype(jnp.int32)


def levels(stream_key, shape, pieces, low, largest):
    def one(dim, blocks):
        steps = jax.random.uniform(jax.random.fold_in(jax.random.fold_in(stream_key, 6), dim), (blocks,), jnp.float32, low / len(pieces), largest / len(pieces))
        return jnp.repeat(jnp.exp(steps), shape[dim] // blocks).reshape((-1,) + (1,) * (len(shape) - dim - 1))

    loudness = one(*pieces[0])
    for cut in pieces[1:]:
        loudness = loudness * one(*cut)
    return loudness


def normal_values(own_key, shape, width, most, shards=(), held_as=jnp.bfloat16):
    level = levels(own_key, shape, shards, -0.22, 0.18) if shards else 1.0
    entries = jax.random.normal(own_key, shape, jnp.float32) * width * level
    return jnp.minimum(jnp.maximum(entries, -most), most).astype(held_as)


def setup_inputs(seed: int = 0) -> dict:
    splits = jax.random.split(jax.random.key(seed), 8)
    fact_features = normal_values(splits[0], (ROWS, DS), 1.0, 6.0, ((0, 768),))
    targets = normal_values(splits[1], (ROWS, OUTS), 1.0, 6.0, ((0, 768),))
    fact_keys = draw_fact_keys(jax.random.fold_in(splits[7], 71), 0)
    fill_counts = draw_fill_counts(jax.random.fold_in(splits[7], 71), 0)
    dim_features = normal_values(splits[4], (DIM_KEYS, DR), 1.0, 6.0, ((0, 768),))
    fact_weight = normal_values(splits[5], (DS, OUTS), DS ** -0.5, 0.375)
    dim_weight = normal_values(splits[6], (DR, OUTS), DR ** -0.5, 0.1875)
    return dict(fact_features=fact_features, targets=targets, fact_keys=fact_keys, fill_counts=fill_counts, dim_features=dim_features, fact_weight=fact_weight, dim_weight=dim_weight)


ridge_weight = 4.0


def reference(fact_features, targets, fact_keys, fill_counts, dim_features, fact_weight, dim_weight):
    dim_values = jnp.dot(dim_features, dim_weight, preferred_element_type=jnp.float32).astype(jnp.bfloat16)
    partial_value = jnp.dot(fact_features, fact_weight, preferred_element_type=jnp.float32) - targets.astype(jnp.float32)
    slot_index = jnp.arange(ROWS, dtype=jnp.int32)
    limits = fill_counts[slot_index // (N_KEY * CAP), (slot_index // CAP) % N_KEY]
    live_slots = (slot_index % CAP) < limits
    found_values = jnp.take(dim_values, fact_keys, axis=0).astype(jnp.float32)
    residual = jnp.where(live_slots[:, None], partial_value + found_values, jnp.float32(0.0)).astype(jnp.bfloat16)
    key_sums = jax.ops.segment_sum(residual.astype(jnp.float32), fact_keys, num_segments=DIM_KEYS)
    row_scale = float(ROWS) ** -0.5
    grad_fact = jnp.dot(fact_features.T, residual, preferred_element_type=jnp.float32) * row_scale + ridge_weight * fact_weight.astype(jnp.float32)
    grad_dim = jnp.dot(dim_features.astype(jnp.float32).T, key_sums, precision=lax.Precision.HIGHEST) * row_scale + ridge_weight * dim_weight.astype(jnp.float32)
    return grad_fact, grad_dim
```

```python
import jax
import jax.numpy as jnp
from jax import lax
from jax.sharding import PartitionSpec as P

ridge_weight = 4.0
ring_size = 8


def fact_groups(fact_devices):
    rings = fact_devices // ring_size
    inner = [[ring * ring_size + i for i in range(ring_size)] for ring in range(rings)]
    outer = [[ring * ring_size + i for ring in range(rings)] for i in range(ring_size)]
    return inner, outer


def spread(array, axis, groups=None):
    return lax.all_to_all(
        array, axis, split_axis=0, concat_axis=0, tiled=True, axis_index_groups=groups
    )


def collect(array, axis, copies, groups):
    return spread(jnp.broadcast_to(array[None], (copies, *array.shape)), axis, groups)


def total_over_devices(terms, inner, outer):
    width = terms.shape[1]
    key_devices = lax.axis_size("key")
    part = spread(terms.reshape(key_devices, -1, width), "key").sum(axis=0)
    part = spread(part.reshape(ring_size, -1, width), "fact", inner).sum(axis=0)
    part = collect(part, "fact", len(inner), outer).sum(axis=0)
    part = collect(part, "fact", ring_size, inner).reshape(-1, width)
    return lax.all_gather(part, "key", axis=0, tiled=True)


def on_device(
    fact_features, targets, fact_keys, fill_counts, dim_features, fact_weight, dim_weight
):
    key_devices = lax.axis_size("key")
    fact_devices = lax.axis_size("fact")
    inner, outer = fact_groups(fact_devices)
    slot_count = fact_keys.shape[0]
    bucket_rows = slot_count // key_devices
    own_keys = dim_features.shape[0]
    fact_width = fact_features.shape[1]
    out_width = fact_weight.shape[1]
    bucket_keys = fact_devices * own_keys
    f32, bf16 = jnp.float32, jnp.bfloat16

    rings = len(inner)
    ring_keys = rings * own_keys

    slot = lax.broadcasted_iota(jnp.int32, (key_devices, bucket_rows), 1)
    owner = fact_keys // (own_keys * key_devices)
    places = (owner % ring_size) * ring_keys + (owner // ring_size) * own_keys + fact_keys % own_keys
    codes = jnp.where(slot < fill_counts[0][:, None], places.reshape(key_devices, bucket_rows), -1)
    codes = spread(codes, "key").reshape(slot_count)
    features = spread(fact_features.reshape(key_devices, bucket_rows, fact_width), "key")
    features = features.reshape(slot_count, fact_width)
    goals = spread(targets.reshape(key_devices, bucket_rows, out_width), "key")
    goals = goals.reshape(slot_count, out_width)

    rows = collect(dim_features, "fact", rings, outer).reshape(ring_keys, -1)
    values = jnp.dot(rows, dim_weight, preferred_element_type=f32).astype(bf16)
    values = collect(values, "fact", ring_size, inner).reshape(bucket_keys, out_width)

    one_hot = (codes[:, None] == jnp.arange(bucket_keys, dtype=jnp.int32)[None, :]).astype(bf16)
    found = jnp.dot(one_hot, values, preferred_element_type=f32)
    partial_value = jnp.dot(features, fact_weight, preferred_element_type=f32) - goals.astype(f32)
    residual = jnp.where(codes[:, None] >= 0, partial_value + found, f32(0.0)).astype(bf16)

    contract = (((0,), (0,)), ((), ()))
    fact_term = lax.dot_general(features, residual, contract, preferred_element_type=f32)
    key_sums = lax.dot_general(one_hot, residual, contract, preferred_element_type=f32)
    key_sums = spread(key_sums.reshape(ring_size, ring_keys, out_width), "fact", inner).sum(axis=0)
    high = key_sums.astype(bf16)
    low = (key_sums - high.astype(f32)).astype(bf16)
    dim_term = lax.dot_general(rows, high, contract, preferred_element_type=f32)
    dim_term = dim_term + lax.dot_general(rows, low, contract, preferred_element_type=f32)

    totals = total_over_devices(jnp.concatenate([fact_term, dim_term], axis=0), inner, outer)
    total_rows = slot_count * fact_devices * key_devices
    row_scale = float(total_rows) ** (-0.5)
    grad_fact = totals[:fact_width] * row_scale + ridge_weight * fact_weight.astype(f32)
    grad_dim = totals[fact_width:] * row_scale + ridge_weight * dim_weight.astype(f32)
    return (grad_fact, grad_dim)


def solution(mesh):
    placed = (
        P(("fact", "key"), None),
        P(("fact", "key"), None),
        P(("fact", "key")),
        P(("fact", "key"), None),
        P(("fact", "key"), None),
        P(),
        P(),
    )
    return jax.shard_map(
        on_device, mesh=mesh, in_specs=placed, out_specs=(P(), P()), check_vma=False
    )
```

```python
import jax
import jax.numpy as jnp
from jax import lax
from jax.sharding import PartitionSpec as P

ridge_weight = 4.0
ring_size = 8
digit = 64
code_rows = 8


def fact_groups(fact_devices):
    rings = fact_devices // ring_size
    inner = [[ring * ring_size + i for i in range(ring_size)] for ring in range(rings)]
    outer = [[ring * ring_size + i for ring in range(rings)] for i in range(ring_size)]
    return inner, outer


def spread(array, axis, groups=None):
    return lax.all_to_all(
        array, axis, split_axis=0, concat_axis=0, tiled=True, axis_index_groups=groups
    )


def collect(array, axis, copies, groups):
    return spread(jnp.broadcast_to(array[None], (copies, *array.shape)), axis, groups)


def total_over_devices(terms, inner, outer):
    width = terms.shape[1]
    key_devices = lax.axis_size("key")
    part = spread(terms.reshape(key_devices, -1, width), "key").sum(axis=0)
    part = spread(part.reshape(ring_size, -1, width), "fact", inner).sum(axis=0)
    part = collect(part, "fact", len(inner), outer).sum(axis=0)
    part = collect(part, "fact", ring_size, inner).reshape(-1, width)
    return lax.all_gather(part, "key", axis=0, tiled=True)


def on_device(
    fact_features, targets, fact_keys, fill_counts, dim_features, fact_weight, dim_weight
):
    key_devices = lax.axis_size("key")
    fact_devices = lax.axis_size("fact")
    inner, outer = fact_groups(fact_devices)
    slot_count = fact_keys.shape[0]
    bucket_rows = slot_count // key_devices
    own_keys = dim_features.shape[0]
    fact_width = fact_features.shape[1]
    out_width = fact_weight.shape[1]
    bucket_keys = fact_devices * own_keys
    f32, bf16 = jnp.float32, jnp.bfloat16

    rings = len(inner)
    ring_keys = rings * own_keys

    slot = lax.broadcasted_iota(jnp.int32, (key_devices, bucket_rows), 1)
    owner = fact_keys // (own_keys * key_devices)
    places = (owner % ring_size) * ring_keys + (owner // ring_size) * own_keys + fact_keys % own_keys
    codes = jnp.where(slot < fill_counts[0][:, None], places.reshape(key_devices, bucket_rows), -digit)
    digits = jnp.concatenate([codes // digit, codes % digit, jnp.zeros_like(codes)], axis=1)
    digits = jnp.pad(digits.astype(bf16)[:, None, :], ((0, 0), (0, code_rows - 1), (0, 0)))
    packed = jnp.concatenate([fact_features, targets], axis=1)
    packed = packed.reshape(key_devices, bucket_rows, fact_width + out_width)
    packed = spread(jnp.concatenate([packed, digits], axis=1), "key")
    slots = packed[:, :bucket_rows].reshape(slot_count, fact_width + out_width)
    features, goals = slots[:, :fact_width], slots[:, fact_width:]
    digits = packed[:, bucket_rows].astype(jnp.int32)
    codes = digits[:, :bucket_rows] * digit + digits[:, bucket_rows : 2 * bucket_rows]
    codes = codes.reshape(slot_count)

    rows = lax.all_gather(dim_features, "fact", axis=0, tiled=True, axis_index_groups=outer)
    values = jnp.dot(rows, dim_weight, preferred_element_type=f32).astype(bf16)
    values = collect(values, "fact", ring_size, inner).reshape(bucket_keys, out_width)

    one_hot = (codes[:, None] == jnp.arange(bucket_keys, dtype=jnp.int32)[None, :]).astype(bf16)
    found = jnp.dot(one_hot, values, preferred_element_type=f32)
    partial_value = jnp.dot(features, fact_weight, preferred_element_type=f32) - goals.astype(f32)
    residual = jnp.where(codes[:, None] >= 0, partial_value + found, f32(0.0)).astype(bf16)

    contract = (((0,), (0,)), ((), ()))
    fact_term = lax.dot_general(features, residual, contract, preferred_element_type=f32)
    key_sums = lax.dot_general(one_hot, residual, contract, preferred_element_type=f32)
    key_sums = spread(key_sums.reshape(ring_size, ring_keys, out_width), "fact", inner).sum(axis=0)
    high = key_sums.astype(bf16)
    low = (key_sums - high.astype(f32)).astype(bf16)
    dim_term = lax.dot_general(rows, high, contract, preferred_element_type=f32)
    dim_term = dim_term + lax.dot_general(rows, low, contract, preferred_element_type=f32)

    totals = total_over_devices(jnp.concatenate([fact_term, dim_term], axis=0), inner, outer)
    total_rows = slot_count * fact_devices * key_devices
    row_scale = float(total_rows) ** (-0.5)
    grad_fact = totals[:fact_width] * row_scale + ridge_weight * fact_weight.astype(f32)
    grad_dim = totals[fact_width:] * row_scale + ridge_weight * dim_weight.astype(f32)
    return (grad_fact, grad_dim)


def solution(mesh):
    placed = (
        P(("fact", "key"), None),
        P(("fact", "key"), None),
        P(("fact", "key")),
        P(("fact", "key"), None),
        P(("fact", "key"), None),
        P(),
        P(),
    )
    return jax.shard_map(
        on_device, mesh=mesh, in_specs=placed, out_specs=(P(), P()), check_vma=False
    )
```

```python
import functools

import jax
import jax.numpy as jnp
from jax import lax
from jax.experimental import pallas as pl
from jax.experimental.pallas import tpu as pltpu
from jax.sharding import PartitionSpec as P

ridge_weight = 4.0
ring_size = 8
digit = 64
extra_rows = 8
f32, bf16, i32 = jnp.float32, jnp.bfloat16, jnp.int32


def fact_groups(fact_devices):
    rings = fact_devices // ring_size
    inner = [[ring * ring_size + i for i in range(ring_size)] for ring in range(rings)]
    outer = [[ring * ring_size + i for ring in range(rings)] for i in range(ring_size)]
    return inner, outer


def spread(array, axis, groups=None):
    return lax.all_to_all(
        array, axis, split_axis=0, concat_axis=0, tiled=True, axis_index_groups=groups
    )


def collect(array, axis, copies, groups):
    return spread(jnp.broadcast_to(array[None], (copies, *array.shape)), axis, groups)


def total_over_devices(terms, inner, outer):
    width = terms.shape[1]
    key_devices = lax.axis_size("key")
    part = spread(terms.reshape(key_devices, -1, width), "key").sum(axis=0)
    part = spread(part.reshape(ring_size, -1, width), "fact", inner).sum(axis=0)
    part = collect(part, "fact", len(inner), outer).sum(axis=0)
    part = collect(part, "fact", ring_size, inner).reshape(-1, width)
    return lax.all_gather(part, "key", axis=0, tiled=True)


def pack_slots(own_keys, ring_keys, keys_ref, fill_ref, features_ref, targets_ref, out_ref):
    buckets, bucket_rows = keys_ref.shape
    width, out_width = features_ref.shape[1], targets_ref.shape[1]
    keys = keys_ref[...]
    owner = keys // (own_keys * buckets)
    places = (owner % ring_size) * ring_keys + (owner // ring_size) * own_keys + keys % own_keys
    slot = lax.broadcasted_iota(i32, (1, bucket_rows), 1)
    for b in range(buckets):
        codes = jnp.where(slot < fill_ref[0, b], places[b : b + 1], -digit)
        high = codes // digit
        low = codes - high * digit
        rows = pl.ds(b * bucket_rows, bucket_rows)
        out_ref[b, pl.ds(0, bucket_rows), pl.ds(0, width)] = features_ref[rows, :]
        out_ref[b, pl.ds(0, bucket_rows), pl.ds(width, out_width)] = targets_ref[rows, :]
        digits = jnp.concatenate([high, low, jnp.zeros_like(high)], axis=1).astype(f32)
        digits = jnp.broadcast_to(digits, (extra_rows, width + out_width))
        out_ref[b, pl.ds(bucket_rows, extra_rows), :] = digits.astype(bf16)


def codes_of(packed_ref, b):
    bucket_rows = packed_ref.shape[1] - extra_rows
    digits = packed_ref[b, pl.ds(bucket_rows, extra_rows), :].astype(f32)
    codes = digits[:, :bucket_rows] * digit + digits[:, bucket_rows : 2 * bucket_rows]
    return codes.astype(i32)[:1]


def partial_of(packed_ref, weight_ref, b):
    bucket_rows = packed_ref.shape[1] - extra_rows
    width = weight_ref.shape[0]
    slots = packed_ref[b, pl.ds(0, bucket_rows), :]
    features = slots[:, :width]
    value = jnp.dot(features, weight_ref[...], preferred_element_type=f32)
    return features, value - slots[:, width:].astype(f32)


def sum_by_key(packed_ref, weight_ref, rows_ref, dim_weight_ref, out_ref):
    members, _, two_widths = out_ref.shape
    out_width = two_widths // 2
    ring_keys = rows_ref.shape[0]
    buckets = packed_ref.shape[0]
    bucket_rows = packed_ref.shape[1] - extra_rows
    places = lax.broadcasted_iota(i32, (members * ring_keys, bucket_rows), 0)
    ones = jnp.ones((extra_rows, bucket_rows), bf16)
    sums = jnp.zeros((members * ring_keys, out_width), f32)
    counts = jnp.zeros((extra_rows, members * ring_keys), f32)
    for b in range(buckets):
        one_hot = jnp.where(places == codes_of(packed_ref, b), f32(1.0), f32(0.0)).astype(bf16)
        _, value = partial_of(packed_ref, weight_ref, b)
        sums += jnp.dot(one_hot, value.astype(bf16), preferred_element_type=f32)
        counts += lax.dot_general(
            ones, one_hot, (((1,), (1,)), ((), ())), preferred_element_type=f32
        )
    values = jnp.dot(rows_ref[...], dim_weight_ref[...], preferred_element_type=f32).astype(bf16)
    high = jnp.floor(counts * (1.0 / digit))
    low = counts - high * digit
    rest = jnp.zeros((extra_rows, out_width - ring_keys), f32)
    for m in range(members):
        own = pl.ds(0, ring_keys)
        part = slice(m * ring_keys, (m + 1) * ring_keys)
        out_ref[m, own, pl.ds(0, out_width)] = sums[part].astype(bf16)
        out_ref[m, own, pl.ds(out_width, out_width)] = values
        digits = jnp.concatenate([high[:, part], rest, low[:, part], rest], axis=1)
        out_ref[m, pl.ds(ring_keys, extra_rows), :] = digits.astype(bf16)


def both_terms(packed_ref, weight_ref, rows_ref, met_ref, out_ref):
    members, _, two_widths = met_ref.shape
    out_width = two_widths // 2
    ring_keys = rows_ref.shape[0]
    buckets = packed_ref.shape[0]
    bucket_rows = packed_ref.shape[1] - extra_rows
    width = weight_ref.shape[0]
    contract = (((0,), (0,)), ((), ()))

    own = pl.ds(0, ring_keys)
    values = jnp.concatenate(
        [met_ref[m, own, pl.ds(out_width, out_width)] for m in range(members)], axis=0
    )
    codes = jnp.concatenate([codes_of(packed_ref, b) for b in range(buckets)], axis=0)
    codes = jnp.transpose(codes.astype(f32)).astype(i32)
    places = lax.broadcasted_iota(i32, (bucket_rows, members * ring_keys), 1)
    fact_term = jnp.zeros((width, out_width), f32)
    for b in range(buckets):
        code = codes[:, b : b + 1]
        one_hot = jnp.where(places == code, f32(1.0), f32(0.0)).astype(bf16)
        features, value = partial_of(packed_ref, weight_ref, b)
        found = jnp.dot(one_hot, values, preferred_element_type=f32)
        residual = jnp.where(code >= 0, value + found, f32(0.0)).astype(bf16)
        fact_term += lax.dot_general(features, residual, contract, preferred_element_type=f32)
    out_ref[pl.ds(0, width), :] = fact_term

    me = lax.rem(lax.axis_index("fact"), ring_size)
    sums = jnp.zeros((ring_keys, out_width), f32)
    digits = jnp.zeros((extra_rows, two_widths), f32)
    for m in range(members):
        sums += met_ref[m, own, pl.ds(0, out_width)].astype(f32)
        digits += met_ref[m, pl.ds(ring_keys, extra_rows), :].astype(f32)
    counts = digits[:1, :out_width] * digit + digits[:1, out_width:]
    diagonal = lax.broadcasted_iota(i32, (ring_keys, out_width), 0) == lax.broadcasted_iota(
        i32, (ring_keys, out_width), 1
    )
    counts = jnp.sum(jnp.where(diagonal, counts, f32(0.0)), axis=1, keepdims=True)
    sums += counts * met_ref[me, own, pl.ds(out_width, out_width)].astype(f32)
    high = sums.astype(bf16)
    low = (sums - high.astype(f32)).astype(bf16)
    dim_term = lax.dot_general(
        rows_ref[...], jnp.concatenate([high, low], axis=1), contract, preferred_element_type=f32
    )
    out_ref[pl.ds(width, rows_ref.shape[1]), :] = dim_term[:, :out_width] + dim_term[:, out_width:]


def kernel_call(body, out_shape, dtype, *operands, smem=()):
    spaces = [pltpu.SMEM if i in smem else pltpu.VMEM for i in range(len(operands))]
    return pl.pallas_call(
        body,
        out_shape=jax.ShapeDtypeStruct(out_shape, dtype),
        in_specs=[pl.BlockSpec(memory_space=space) for space in spaces],
        out_specs=pl.BlockSpec(memory_space=pltpu.VMEM),
        compiler_params=pltpu.CompilerParams(vmem_limit_bytes=32 << 20),
    )(*operands)


def on_device(
    fact_features, targets, fact_keys, fill_counts, dim_features, fact_weight, dim_weight
):
    key_devices = lax.axis_size("key")
    fact_devices = lax.axis_size("fact")
    inner, outer = fact_groups(fact_devices)
    slot_count = fact_keys.shape[0]
    bucket_rows = slot_count // key_devices
    own_keys, dim_width = dim_features.shape
    fact_width, out_width = fact_weight.shape
    ring_keys = len(inner) * own_keys

    packed = kernel_call(
        functools.partial(pack_slots, own_keys, ring_keys),
        (key_devices, bucket_rows + extra_rows, fact_width + out_width),
        bf16,
        fact_keys.reshape(key_devices, bucket_rows),
        fill_counts,
        fact_features,
        targets,
        smem=(1,),
    )
    packed = spread(packed, "key")
    rows = lax.all_gather(dim_features, "fact", axis=0, tiled=True, axis_index_groups=outer)

    met = kernel_call(
        sum_by_key,
        (ring_size, ring_keys + extra_rows, 2 * out_width),
        bf16,
        packed,
        fact_weight,
        rows,
        dim_weight,
    )
    met = spread(met, "fact", inner)
    terms = kernel_call(
        both_terms, (fact_width + dim_width, out_width), f32, packed, fact_weight, rows, met
    )

    totals = total_over_devices(terms, inner, outer)
    total_rows = slot_count * fact_devices * key_devices
    row_scale = float(total_rows) ** (-0.5)
    grad_fact = totals[:fact_width] * row_scale + ridge_weight * fact_weight.astype(f32)
    grad_dim = totals[fact_width:] * row_scale + ridge_weight * dim_weight.astype(f32)
    return (grad_fact, grad_dim)


def solution(mesh):
    placed = (
        P(("fact", "key"), None),
        P(("fact", "key"), None),
        P(("fact", "key")),
        P(("fact", "key"), None),
        P(("fact", "key"), None),
        P(),
        P(),
    )
    return jax.shard_map(
        on_device, mesh=mesh, in_specs=placed, out_specs=(P(), P()), check_vma=False
    )
```

```python
import functools

import jax
import jax.numpy as jnp
from jax import lax
from jax.experimental import pallas as pl
from jax.experimental.pallas import tpu as pltpu
from jax.sharding import PartitionSpec as P

ridge_weight = 4.0
ring_size = 8
digit = 64
extra_rows = 8
f32, bf16, i32 = jnp.float32, jnp.bfloat16, jnp.int32


def groups_of(fact_devices, key_devices):
    levels = range(fact_devices // ring_size)
    chips, cores = range(key_devices // 2), range(2)
    one_z = [[z * ring_size + y for y in range(ring_size)] for z in levels]
    one_y = [[z * ring_size + y for z in levels] for y in range(ring_size)]
    chip = [[2 * x + core for core in cores] for x in chips]
    plane = [
        [(z * ring_size + y) * key_devices + 2 * x + core for y in range(ring_size) for x in chips]
        for z in levels
        for core in cores
    ]
    return one_z, one_y, chip, plane


def spread(array, axis, groups=None):
    return lax.all_to_all(
        array, axis, split_axis=0, concat_axis=0, tiled=True, axis_index_groups=groups
    )


def collect(array, axis, copies, groups):
    return spread(jnp.broadcast_to(array[None], (copies, *array.shape)), axis, groups)


def total_over_devices(terms, one_y, chip, plane):
    width = terms.shape[1]
    both = ("fact", "key")
    members = len(plane[0])
    part = spread(terms.reshape(2, -1, width), "key", chip).sum(axis=0)
    part = spread(part.reshape(members, -1, width), both, plane).sum(axis=0)
    part = collect(part, "fact", len(one_y[0]), one_y).sum(axis=0)
    part = collect(part, both, members, plane).reshape(-1, width)
    return lax.all_gather(part, "key", axis=0, tiled=True, axis_index_groups=chip)


def pack_slots(
    own_keys, ring_keys, keys_hbm, fill_hbm, features_hbm, targets_hbm, out_hbm, keys_ref, fill_ref, rows_ref, done
):
    buckets, bucket_rows, width = features_hbm.shape
    out_width = targets_hbm.shape[2]
    slots = pl.ds(0, bucket_rows)
    copies = [
        pltpu.make_async_copy(keys_hbm, keys_ref, done.at[0]),
        pltpu.make_async_copy(fill_hbm, fill_ref, done.at[1]),
        pltpu.make_async_copy(features_hbm, out_hbm.at[:, slots, pl.ds(0, width)], done.at[2]),
        pltpu.make_async_copy(targets_hbm, out_hbm.at[:, slots, pl.ds(width, out_width)], done.at[3]),
        pltpu.make_async_copy(rows_ref, out_hbm.at[:, pl.ds(bucket_rows, extra_rows), :], done.at[4]),
    ]
    for copy in copies[:4]:
        copy.start()
    copies[0].wait()
    copies[1].wait()
    keys = keys_ref[...]
    owner = keys // (own_keys * buckets)
    places = (owner % ring_size) * ring_keys + (owner // ring_size) * own_keys + keys % own_keys
    slot = lax.broadcasted_iota(i32, (1, bucket_rows), 1)
    for b in range(buckets):
        codes = jnp.where(slot < fill_ref[0, b], places[b : b + 1], -digit)
        high = codes // digit
        low = codes - high * digit
        digits = jnp.concatenate([high, low, jnp.zeros_like(high)], axis=1).astype(f32)
        rows_ref[b] = jnp.broadcast_to(digits, (extra_rows, width + out_width)).astype(bf16)
    copies[4].start()
    for copy in copies[2:]:
        copy.wait()


def codes_of(packed_ref, b):
    bucket_rows = packed_ref.shape[1] - extra_rows
    digits = packed_ref[b, pl.ds(bucket_rows, extra_rows), :].astype(f32)
    codes = digits[:, :bucket_rows] * digit + digits[:, bucket_rows : 2 * bucket_rows]
    return codes.astype(i32)[:1]


def partial_of(packed_ref, weight_ref, b):
    bucket_rows = packed_ref.shape[1] - extra_rows
    width = weight_ref.shape[0]
    slots = packed_ref[b, pl.ds(0, bucket_rows), :]
    features = slots[:, :width]
    value = jnp.dot(features, weight_ref[...], preferred_element_type=f32)
    return features, value - slots[:, width:].astype(f32)


def sum_by_key(packed_ref, weight_ref, rows_ref, dim_weight_ref, out_ref):
    members, _, two_widths = out_ref.shape
    out_width = two_widths // 2
    ring_keys = rows_ref.shape[0]
    buckets = packed_ref.shape[0]
    bucket_rows = packed_ref.shape[1] - extra_rows
    places = lax.broadcasted_iota(i32, (members * ring_keys, bucket_rows), 0)
    ones = jnp.ones((extra_rows, bucket_rows), bf16)
    sums = jnp.zeros((members * ring_keys, out_width), f32)
    counts = jnp.zeros((extra_rows, members * ring_keys), f32)
    for b in range(buckets):
        one_hot = jnp.where(places == codes_of(packed_ref, b), f32(1.0), f32(0.0)).astype(bf16)
        _, value = partial_of(packed_ref, weight_ref, b)
        sums += jnp.dot(one_hot, value.astype(bf16), preferred_element_type=f32)
        counts += lax.dot_general(
            ones, one_hot, (((1,), (1,)), ((), ())), preferred_element_type=f32
        )
    values = jnp.dot(rows_ref[...], dim_weight_ref[...], preferred_element_type=f32).astype(bf16)
    high = jnp.floor(counts * (1.0 / digit))
    low = counts - high * digit
    rest = jnp.zeros((extra_rows, out_width - ring_keys), f32)
    for m in range(members):
        own = pl.ds(0, ring_keys)
        part = slice(m * ring_keys, (m + 1) * ring_keys)
        out_ref[m, own, pl.ds(0, out_width)] = sums[part].astype(bf16)
        out_ref[m, own, pl.ds(out_width, out_width)] = values
        digits = jnp.concatenate([high[:, part], rest, low[:, part], rest], axis=1)
        out_ref[m, pl.ds(ring_keys, extra_rows), :] = digits.astype(bf16)


def both_terms(packed_ref, weight_ref, rows_ref, met_ref, out_ref):
    members, _, two_widths = met_ref.shape
    out_width = two_widths // 2
    ring_keys = rows_ref.shape[0]
    buckets = packed_ref.shape[0]
    bucket_rows = packed_ref.shape[1] - extra_rows
    width = weight_ref.shape[0]
    contract = (((0,), (0,)), ((), ()))

    own = pl.ds(0, ring_keys)
    values = jnp.concatenate(
        [met_ref[m, own, pl.ds(out_width, out_width)] for m in range(members)], axis=0
    )
    codes = jnp.concatenate([codes_of(packed_ref, b) for b in range(buckets)], axis=0)
    codes = jnp.transpose(codes.astype(f32)).astype(i32)
    places = lax.broadcasted_iota(i32, (bucket_rows, members * ring_keys), 1)
    fact_term = jnp.zeros((width, out_width), f32)
    for b in range(buckets):
        code = codes[:, b : b + 1]
        one_hot = jnp.where(places == code, f32(1.0), f32(0.0)).astype(bf16)
        features, value = partial_of(packed_ref, weight_ref, b)
        found = jnp.dot(one_hot, values, preferred_element_type=f32)
        residual = jnp.where(code >= 0, value + found, f32(0.0)).astype(bf16)
        fact_term += lax.dot_general(features, residual, contract, preferred_element_type=f32)
    out_ref[pl.ds(0, width), :] = fact_term

    me = lax.rem(lax.axis_index("fact"), ring_size)
    sums = jnp.zeros((ring_keys, out_width), f32)
    digits = jnp.zeros((extra_rows, two_widths), f32)
    for m in range(members):
        sums += met_ref[m, own, pl.ds(0, out_width)].astype(f32)
        digits += met_ref[m, pl.ds(ring_keys, extra_rows), :].astype(f32)
    counts = digits[:1, :out_width] * digit + digits[:1, out_width:]
    diagonal = lax.broadcasted_iota(i32, (ring_keys, out_width), 0) == lax.broadcasted_iota(
        i32, (ring_keys, out_width), 1
    )
    counts = jnp.sum(jnp.where(diagonal, counts, f32(0.0)), axis=1, keepdims=True)
    sums += counts * met_ref[me, own, pl.ds(out_width, out_width)].astype(f32)
    high = sums.astype(bf16)
    low = (sums - high.astype(f32)).astype(bf16)
    dim_term = lax.dot_general(
        rows_ref[...], jnp.concatenate([high, low], axis=1), contract, preferred_element_type=f32
    )
    out_ref[pl.ds(width, rows_ref.shape[1]), :] = dim_term[:, :out_width] + dim_term[:, out_width:]


def kernel_call(body, out_shape, dtype, *operands):
    return pl.pallas_call(
        body,
        out_shape=jax.ShapeDtypeStruct(out_shape, dtype),
        in_specs=[pl.BlockSpec(memory_space=pltpu.VMEM)] * len(operands),
        out_specs=pl.BlockSpec(memory_space=pltpu.VMEM),
        compiler_params=pltpu.CompilerParams(vmem_limit_bytes=32 << 20),
    )(*operands)


def on_device(
    fact_features, targets, fact_keys, fill_counts, dim_features, fact_weight, dim_weight
):
    key_devices = lax.axis_size("key")
    fact_devices = lax.axis_size("fact")
    one_z, one_y, chip, plane = groups_of(fact_devices, key_devices)
    slot_count = fact_keys.shape[0]
    bucket_rows = slot_count // key_devices
    own_keys, dim_width = dim_features.shape
    fact_width, out_width = fact_weight.shape
    ring_keys = len(one_z) * own_keys

    packed = pl.pallas_call(
        functools.partial(pack_slots, own_keys, ring_keys),
        out_shape=jax.ShapeDtypeStruct(
            (key_devices, bucket_rows + extra_rows, fact_width + out_width), bf16
        ),
        in_specs=[pl.BlockSpec(memory_space=pl.ANY)] * 4,
        out_specs=pl.BlockSpec(memory_space=pl.ANY),
        scratch_shapes=[
            pltpu.VMEM((key_devices, bucket_rows), i32),
            pltpu.SMEM((1, key_devices), i32),
            pltpu.VMEM((key_devices, extra_rows, fact_width + out_width), bf16),
            pltpu.SemaphoreType.DMA((5,)),
        ],
    )(
        fact_keys.reshape(key_devices, bucket_rows),
        fill_counts,
        fact_features.reshape(key_devices, bucket_rows, fact_width),
        targets.reshape(key_devices, bucket_rows, out_width),
    )
    packed = spread(packed, "key")
    rows = lax.all_gather(dim_features, "fact", axis=0, tiled=True, axis_index_groups=one_y)

    met = kernel_call(
        sum_by_key,
        (ring_size, ring_keys + extra_rows, 2 * out_width),
        bf16,
        packed,
        fact_weight,
        rows,
        dim_weight,
    )
    met = spread(met, "fact", one_z)
    terms = kernel_call(
        both_terms, (fact_width + dim_width, out_width), f32, packed, fact_weight, rows, met
    )

    totals = total_over_devices(terms, one_y, chip, plane)
    total_rows = slot_count * fact_devices * key_devices
    row_scale = float(total_rows) ** (-0.5)
    grad_fact = totals[:fact_width] * row_scale + ridge_weight * fact_weight.astype(f32)
    grad_dim = totals[fact_width:] * row_scale + ridge_weight * dim_weight.astype(f32)
    return (grad_fact, grad_dim)


def solution(mesh):
    placed = (
        P(("fact", "key"), None),
        P(("fact", "key"), None),
        P(("fact", "key")),
        P(("fact", "key"), None),
        P(("fact", "key"), None),
        P(),
        P(),
    )
    return jax.shard_map(
        on_device, mesh=mesh, in_specs=placed, out_specs=(P(), P()), check_vma=False
    )
```

```python
import functools

import jax
import jax.numpy as jnp
from jax import lax
from jax.experimental import pallas as pl
from jax.experimental.pallas import tpu as pltpu
from jax.sharding import PartitionSpec as P

ridge_weight = 4.0
ring_size = 8
digit = 64
extra_rows = 8
f32, bf16, i32 = jnp.float32, jnp.bfloat16, jnp.int32


def groups_of(fact_devices, key_devices):
    levels = range(fact_devices // ring_size)
    chips, cores = range(key_devices // 2), range(2)
    one_z = [[z * ring_size + y for y in range(ring_size)] for z in levels]
    one_y = [[z * ring_size + y for z in levels] for y in range(ring_size)]
    chip = [[2 * x + core for core in cores] for x in chips]
    plane = [
        [(z * ring_size + y) * key_devices + 2 * x + core for y in range(ring_size) for x in chips]
        for z in levels
        for core in cores
    ]
    return one_z, one_y, chip, plane


def spread(array, axis, groups=None):
    return lax.all_to_all(
        array, axis, split_axis=0, concat_axis=0, tiled=True, axis_index_groups=groups
    )


def collect(array, axis, copies, groups):
    return spread(jnp.broadcast_to(array[None], (copies, *array.shape)), axis, groups)


def total_over_devices(terms, one_y, chip, plane):
    width = terms.shape[1]
    both = ("fact", "key")
    members = len(plane[0])
    part = spread(terms.reshape(2, -1, width), "key", chip).sum(axis=0)
    part = spread(part.reshape(members, -1, width), both, plane).sum(axis=0)
    part = collect(part, "fact", len(one_y[0]), one_y).sum(axis=0)
    part = collect(part, both, members, plane).reshape(-1, width)
    return lax.all_gather(part, "key", axis=0, tiled=True, axis_index_groups=chip)


def pack_slots(
    own_keys, ring_keys, keys_hbm, fill_hbm, features_hbm, targets_hbm, out_ref, keys_ref, fill_ref, done
):
    buckets, bucket_rows, width = features_hbm.shape
    out_width = targets_hbm.shape[2]
    slots = pl.ds(0, bucket_rows)
    copies = [
        pltpu.make_async_copy(keys_hbm, keys_ref, done.at[0]),
        pltpu.make_async_copy(fill_hbm, fill_ref, done.at[1]),
        pltpu.make_async_copy(features_hbm, out_ref.at[:, slots, pl.ds(0, width)], done.at[2]),
        pltpu.make_async_copy(targets_hbm, out_ref.at[:, slots, pl.ds(width, out_width)], done.at[3]),
    ]
    for copy in copies:
        copy.start()
    copies[0].wait()
    copies[1].wait()
    keys = keys_ref[...]
    owner = keys // (own_keys * buckets)
    places = (owner % ring_size) * ring_keys + (owner // ring_size) * own_keys + keys % own_keys
    slot = lax.broadcasted_iota(i32, (1, bucket_rows), 1)
    for b in range(buckets):
        codes = jnp.where(slot < fill_ref[0, b], places[b : b + 1], -digit)
        high = codes // digit
        low = codes - high * digit
        digits = jnp.concatenate([high, low, jnp.zeros_like(high)], axis=1).astype(f32)
        digits = jnp.broadcast_to(digits, (extra_rows, width + out_width))
        out_ref[b, pl.ds(bucket_rows, extra_rows), :] = digits.astype(bf16)
    for copy in copies[2:]:
        copy.wait()


def codes_of(packed_ref, b):
    bucket_rows = packed_ref.shape[1] - extra_rows
    digits = packed_ref[b, pl.ds(bucket_rows, extra_rows), :].astype(f32)
    codes = digits[:, :bucket_rows] * digit + digits[:, bucket_rows : 2 * bucket_rows]
    return codes.astype(i32)[:1]


def partial_of(packed_ref, weight_ref, b):
    bucket_rows = packed_ref.shape[1] - extra_rows
    width = weight_ref.shape[0]
    slots = packed_ref[b, pl.ds(0, bucket_rows), :]
    features = slots[:, :width]
    value = jnp.dot(features, weight_ref[...], preferred_element_type=f32)
    return features, value - slots[:, width:].astype(f32)


def sum_by_key(packed_ref, weight_ref, rows_ref, dim_weight_ref, out_ref):
    members, _, two_widths = out_ref.shape
    out_width = two_widths // 2
    ring_keys = rows_ref.shape[0]
    buckets = packed_ref.shape[0]
    bucket_rows = packed_ref.shape[1] - extra_rows
    places = lax.broadcasted_iota(i32, (members * ring_keys, bucket_rows), 0)
    ones = jnp.ones((extra_rows, bucket_rows), bf16)
    sums = jnp.zeros((members * ring_keys, out_width), f32)
    counts = jnp.zeros((extra_rows, members * ring_keys), f32)
    for b in range(buckets):
        one_hot = jnp.where(places == codes_of(packed_ref, b), f32(1.0), f32(0.0)).astype(bf16)
        _, value = partial_of(packed_ref, weight_ref, b)
        sums += jnp.dot(one_hot, value.astype(bf16), preferred_element_type=f32)
        counts += lax.dot_general(
            ones, one_hot, (((1,), (1,)), ((), ())), preferred_element_type=f32
        )
    values = jnp.dot(rows_ref[...], dim_weight_ref[...], preferred_element_type=f32).astype(bf16)
    high = jnp.floor(counts * (1.0 / digit))
    low = counts - high * digit
    rest = jnp.zeros((extra_rows, out_width - ring_keys), f32)
    for m in range(members):
        own = pl.ds(0, ring_keys)
        part = slice(m * ring_keys, (m + 1) * ring_keys)
        out_ref[m, own, pl.ds(0, out_width)] = sums[part].astype(bf16)
        out_ref[m, own, pl.ds(out_width, out_width)] = values
        digits = jnp.concatenate([high[:, part], rest, low[:, part], rest], axis=1)
        out_ref[m, pl.ds(ring_keys, extra_rows), :] = digits.astype(bf16)


def both_terms(packed_ref, weight_ref, rows_ref, met_ref, out_ref):
    members, _, two_widths = met_ref.shape
    out_width = two_widths // 2
    ring_keys = rows_ref.shape[0]
    buckets = packed_ref.shape[0]
    bucket_rows = packed_ref.shape[1] - extra_rows
    width = weight_ref.shape[0]
    contract = (((0,), (0,)), ((), ()))

    own = pl.ds(0, ring_keys)
    values = jnp.concatenate(
        [met_ref[m, own, pl.ds(out_width, out_width)] for m in range(members)], axis=0
    )
    codes = jnp.concatenate([codes_of(packed_ref, b) for b in range(buckets)], axis=0)
    codes = jnp.transpose(codes.astype(f32)).astype(i32)
    places = lax.broadcasted_iota(i32, (bucket_rows, members * ring_keys), 1)
    fact_term = jnp.zeros((width, out_width), f32)
    for b in range(buckets):
        code = codes[:, b : b + 1]
        one_hot = jnp.where(places == code, f32(1.0), f32(0.0)).astype(bf16)
        features, value = partial_of(packed_ref, weight_ref, b)
        found = jnp.dot(one_hot, values, preferred_element_type=f32)
        residual = jnp.where(code >= 0, value + found, f32(0.0)).astype(bf16)
        fact_term += lax.dot_general(features, residual, contract, preferred_element_type=f32)
    out_ref[pl.ds(0, width), :] = fact_term

    me = lax.rem(lax.axis_index("fact"), ring_size)
    sums = jnp.zeros((ring_keys, out_width), f32)
    digits = jnp.zeros((extra_rows, two_widths), f32)
    for m in range(members):
        sums += met_ref[m, own, pl.ds(0, out_width)].astype(f32)
        digits += met_ref[m, pl.ds(ring_keys, extra_rows), :].astype(f32)
    counts = digits[:1, :out_width] * digit + digits[:1, out_width:]
    diagonal = lax.broadcasted_iota(i32, (ring_keys, out_width), 0) == lax.broadcasted_iota(
        i32, (ring_keys, out_width), 1
    )
    counts = jnp.sum(jnp.where(diagonal, counts, f32(0.0)), axis=1, keepdims=True)
    sums += counts * met_ref[me, own, pl.ds(out_width, out_width)].astype(f32)
    high = sums.astype(bf16)
    low = (sums - high.astype(f32)).astype(bf16)
    dim_term = lax.dot_general(
        rows_ref[...], jnp.concatenate([high, low], axis=1), contract, preferred_element_type=f32
    )
    out_ref[pl.ds(width, rows_ref.shape[1]), :] = dim_term[:, :out_width] + dim_term[:, out_width:]


def kernel_call(body, out_shape, dtype, *operands):
    return pl.pallas_call(
        body,
        out_shape=jax.ShapeDtypeStruct(out_shape, dtype),
        in_specs=[pl.BlockSpec(memory_space=pltpu.VMEM)] * len(operands),
        out_specs=pl.BlockSpec(memory_space=pltpu.VMEM),
        compiler_params=pltpu.CompilerParams(vmem_limit_bytes=32 << 20),
    )(*operands)


def on_device(
    fact_features, targets, fact_keys, fill_counts, dim_features, fact_weight, dim_weight
):
    key_devices = lax.axis_size("key")
    fact_devices = lax.axis_size("fact")
    one_z, one_y, chip, plane = groups_of(fact_devices, key_devices)
    slot_count = fact_keys.shape[0]
    bucket_rows = slot_count // key_devices
    own_keys, dim_width = dim_features.shape
    fact_width, out_width = fact_weight.shape
    ring_keys = len(one_z) * own_keys

    packed = pl.pallas_call(
        functools.partial(pack_slots, own_keys, ring_keys),
        out_shape=jax.ShapeDtypeStruct(
            (key_devices, bucket_rows + extra_rows, fact_width + out_width), bf16
        ),
        in_specs=[pl.BlockSpec(memory_space=pl.ANY)] * 4,
        out_specs=pl.BlockSpec(memory_space=pltpu.VMEM),
        scratch_shapes=[
            pltpu.VMEM((key_devices, bucket_rows), i32),
            pltpu.SMEM((1, key_devices), i32),
            pltpu.SemaphoreType.DMA((4,)),
        ],
    )(
        fact_keys.reshape(key_devices, bucket_rows),
        fill_counts,
        fact_features.reshape(key_devices, bucket_rows, fact_width),
        targets.reshape(key_devices, bucket_rows, out_width),
    )
    packed = spread(packed, "key")
    rows = lax.all_gather(dim_features, "fact", axis=0, tiled=True, axis_index_groups=one_y)

    met = kernel_call(
        sum_by_key,
        (ring_size, ring_keys + extra_rows, 2 * out_width),
        bf16,
        packed,
        fact_weight,
        rows,
        dim_weight,
    )
    met = spread(met, "fact", one_z)
    terms = kernel_call(
        both_terms, (fact_width + dim_width, out_width), f32, packed, fact_weight, rows, met
    )

    totals = total_over_devices(terms, one_y, chip, plane)
    total_rows = slot_count * fact_devices * key_devices
    row_scale = float(total_rows) ** (-0.5)
    grad_fact = totals[:fact_width] * row_scale + ridge_weight * fact_weight.astype(f32)
    grad_dim = totals[fact_width:] * row_scale + ridge_weight * dim_weight.astype(f32)
    return (grad_fact, grad_dim)


def solution(mesh):
    placed = (
        P(("fact", "key"), None),
        P(("fact", "key"), None),
        P(("fact", "key")),
        P(("fact", "key"), None),
        P(("fact", "key"), None),
        P(),
        P(),
    )
    return jax.shard_map(
        on_device, mesh=mesh, in_specs=placed, out_specs=(P(), P()), check_vma=False
    )
```

```python
import functools

import jax
import jax.numpy as jnp
from jax import lax
from jax.experimental import pallas as pl
from jax.experimental.pallas import tpu as pltpu
from jax.sharding import PartitionSpec as P

ridge_weight = 4.0
ring_size = 8
digit = 64
extra_rows = 8
f32, bf16, i32 = jnp.float32, jnp.bfloat16, jnp.int32


def groups_of(fact_devices, key_devices):
    levels = range(fact_devices // ring_size)
    chips, cores = range(key_devices // 2), range(2)
    one_z = [[z * ring_size + y for y in range(ring_size)] for z in levels]
    one_y = [[z * ring_size + y for z in levels] for y in range(ring_size)]
    chip = [[2 * x + core for core in cores] for x in chips]
    plane = [
        [(z * ring_size + y) * key_devices + 2 * x + core for y in range(ring_size) for x in chips]
        for z in levels
        for core in cores
    ]
    return one_z, one_y, chip, plane


def spread(array, axis, groups=None):
    return lax.all_to_all(
        array, axis, split_axis=0, concat_axis=0, tiled=True, axis_index_groups=groups
    )


def collect(array, axis, copies, groups):
    return spread(jnp.broadcast_to(array[None], (copies, *array.shape)), axis, groups)


def total_over_devices(terms, one_y, chip, plane):
    rows, width = terms.shape
    both = ("fact", "key")
    members = len(plane[0])
    part = spread(terms.reshape(2, -1, 4, width), "key", chip).sum(axis=0)
    part = spread(part.reshape(members, -1, 4, width), both, plane).sum(axis=0)
    part = collect(part, "fact", len(one_y[0]), one_y).sum(axis=0)
    part = collect(part, both, members, plane).reshape(-1, 4, width)
    part = lax.all_gather(part, "key", axis=0, tiled=True, axis_index_groups=chip)
    return part.reshape(rows, width)


def pack_slots(
    own_keys, ring_keys, keys_hbm, fill_hbm, features_hbm, targets_hbm, out_ref, keys_ref, fill_ref, done
):
    buckets, bucket_rows, width = features_hbm.shape
    out_width = targets_hbm.shape[2]
    slots = pl.ds(0, bucket_rows)
    copies = [
        pltpu.make_async_copy(keys_hbm, keys_ref, done.at[0]),
        pltpu.make_async_copy(fill_hbm, fill_ref, done.at[1]),
        pltpu.make_async_copy(features_hbm, out_ref.at[:, slots, pl.ds(0, width)], done.at[2]),
        pltpu.make_async_copy(targets_hbm, out_ref.at[:, slots, pl.ds(width, out_width)], done.at[3]),
    ]
    for copy in copies:
        copy.start()
    copies[0].wait()
    copies[1].wait()
    keys = keys_ref[...]
    owner = keys // (own_keys * buckets)
    places = (owner % ring_size) * ring_keys + (owner // ring_size) * own_keys + keys % own_keys
    slot = lax.broadcasted_iota(i32, (1, bucket_rows), 1)
    for b in range(buckets):
        codes = jnp.where(slot < fill_ref[0, b], places[b : b + 1], -digit)
        high = codes // digit
        low = codes - high * digit
        digits = jnp.concatenate([high, low, jnp.zeros_like(high)], axis=1).astype(f32)
        digits = jnp.broadcast_to(digits, (extra_rows, width + out_width))
        out_ref[b, pl.ds(bucket_rows, extra_rows), :] = digits.astype(bf16)
    for copy in copies[2:]:
        copy.wait()


def codes_of(packed_ref, b):
    bucket_rows = packed_ref.shape[1] - extra_rows
    digits = packed_ref[b, pl.ds(bucket_rows, extra_rows), :].astype(f32)
    codes = digits[:, :bucket_rows] * digit + digits[:, bucket_rows : 2 * bucket_rows]
    return codes.astype(i32)[:1]


def partial_of(packed_ref, weight_ref, pair):
    slots = pl.ds(0, packed_ref.shape[1] - extra_rows)
    width = weight_ref.shape[0]
    rows = jnp.concatenate([packed_ref[b, slots, :] for b in pair], axis=0)
    features = rows[:, :width]
    value = jnp.dot(features, weight_ref[...], preferred_element_type=f32)
    return features, value - rows[:, width:].astype(f32)


def pairs_of(packed_ref):
    return [(b, b + 1) for b in range(0, packed_ref.shape[0], 2)]


def diagonal_of(rows, columns):
    return lax.broadcasted_iota(i32, (rows, columns), 0) == lax.broadcasted_iota(
        i32, (rows, columns), 1
    )


def sum_by_key(packed_ref, weight_ref, rows_ref, dim_weight_ref, out_ref):
    members, _, two_widths = out_ref.shape
    out_width = two_widths // 2
    ring_keys = rows_ref.shape[0]
    two_rows = 2 * (packed_ref.shape[1] - extra_rows)
    places = lax.broadcasted_iota(i32, (members * ring_keys, two_rows), 0)
    ones = jnp.ones((two_rows, out_width), bf16)
    sums = jnp.zeros((members * ring_keys, two_widths), f32)
    for pair in pairs_of(packed_ref):
        codes = jnp.concatenate([codes_of(packed_ref, b) for b in pair], axis=1)
        one_hot = jnp.where(places == codes, f32(1.0), f32(0.0)).astype(bf16)
        _, value = partial_of(packed_ref, weight_ref, pair)
        value = jnp.concatenate([value.astype(bf16), ones], axis=1)
        sums += jnp.dot(one_hot, value, preferred_element_type=f32)
    values = jnp.dot(rows_ref[...], dim_weight_ref[...], preferred_element_type=f32).astype(bf16)
    diagonal = diagonal_of(ring_keys, out_width)
    own = pl.ds(0, ring_keys)
    for m in range(members):
        part = sums[m * ring_keys : (m + 1) * ring_keys]
        out_ref[m, own, pl.ds(0, out_width)] = part[:, :out_width].astype(bf16)
        out_ref[m, own, pl.ds(out_width, out_width)] = values
        counts = jnp.where(diagonal, part[:, out_width:], f32(0.0)).sum(axis=0, keepdims=True)
        high = jnp.floor(counts * (1.0 / digit))
        digits = jnp.concatenate([high, counts - high * digit], axis=1)
        digits = jnp.broadcast_to(digits, (extra_rows, two_widths))
        out_ref[m, pl.ds(ring_keys, extra_rows), :] = digits.astype(bf16)


def both_terms(packed_ref, weight_ref, rows_ref, met_ref, out_ref):
    members, _, two_widths = met_ref.shape
    out_width = two_widths // 2
    ring_keys = rows_ref.shape[0]
    buckets = packed_ref.shape[0]
    bucket_rows = packed_ref.shape[1] - extra_rows
    width = weight_ref.shape[0]
    contract = (((0,), (0,)), ((), ()))

    own = pl.ds(0, ring_keys)
    values = jnp.concatenate(
        [met_ref[m, own, pl.ds(out_width, out_width)] for m in range(members)], axis=0
    )
    codes = jnp.concatenate([codes_of(packed_ref, b) for b in range(buckets)], axis=0)
    codes = jnp.transpose(codes.astype(f32)).astype(i32)
    places = lax.broadcasted_iota(i32, (bucket_rows, members * ring_keys), 1)
    fact_term = jnp.zeros((width, out_width), f32)
    for pair in pairs_of(packed_ref):
        one_hot = [
            jnp.where(places == codes[:, b : b + 1], f32(1.0), f32(0.0)).astype(bf16) for b in pair
        ]
        features, value = partial_of(packed_ref, weight_ref, pair)
        found = jnp.dot(jnp.concatenate(one_hot, axis=0), values, preferred_element_type=f32)
        live = jnp.concatenate([codes[:, b : b + 1] for b in pair], axis=0) >= 0
        residual = jnp.where(live, value + found, f32(0.0)).astype(bf16)
        fact_term += lax.dot_general(features, residual, contract, preferred_element_type=f32)
    out_ref[pl.ds(0, width), :] = fact_term

    me = lax.rem(lax.axis_index("fact"), ring_size)
    sums = jnp.zeros((ring_keys, out_width), f32)
    digits = jnp.zeros((extra_rows, two_widths), f32)
    for m in range(members):
        sums += met_ref[m, own, pl.ds(0, out_width)].astype(f32)
        digits += met_ref[m, pl.ds(ring_keys, extra_rows), :].astype(f32)
    counts = digits[:1, :out_width] * digit + digits[:1, out_width:]
    diagonal = diagonal_of(ring_keys, out_width)
    counts = jnp.sum(jnp.where(diagonal, counts, f32(0.0)), axis=1, keepdims=True)
    sums += counts * met_ref[me, own, pl.ds(out_width, out_width)].astype(f32)
    high = sums.astype(bf16)
    low = (sums - high.astype(f32)).astype(bf16)
    dim_term = lax.dot_general(
        rows_ref[...], jnp.concatenate([high, low], axis=1), contract, preferred_element_type=f32
    )
    out_ref[pl.ds(width, rows_ref.shape[1]), :] = dim_term[:, :out_width] + dim_term[:, out_width:]


def finish(row_scale, totals_ref, fact_weight_ref, dim_weight_ref, fact_ref, dim_ref):
    width = fact_ref.shape[0]
    fact_ref[...] = totals_ref[pl.ds(0, width), :] * row_scale + ridge_weight * fact_weight_ref[
        ...
    ].astype(f32)
    dim_ref[...] = totals_ref[
        pl.ds(width, dim_ref.shape[0]), :
    ] * row_scale + ridge_weight * dim_weight_ref[...].astype(f32)


def kernel_call(body, out_shape, dtype, *operands):
    return pl.pallas_call(
        body,
        out_shape=jax.ShapeDtypeStruct(out_shape, dtype),
        in_specs=[pl.BlockSpec(memory_space=pltpu.VMEM)] * len(operands),
        out_specs=pl.BlockSpec(memory_space=pltpu.VMEM),
        compiler_params=pltpu.CompilerParams(vmem_limit_bytes=32 << 20),
    )(*operands)


def on_device(
    fact_features, targets, fact_keys, fill_counts, dim_features, fact_weight, dim_weight
):
    key_devices = lax.axis_size("key")
    fact_devices = lax.axis_size("fact")
    one_z, one_y, chip, plane = groups_of(fact_devices, key_devices)
    slot_count = fact_keys.shape[0]
    bucket_rows = slot_count // key_devices
    own_keys, dim_width = dim_features.shape
    fact_width, out_width = fact_weight.shape
    ring_keys = len(one_z) * own_keys

    packed = pl.pallas_call(
        functools.partial(pack_slots, own_keys, ring_keys),
        out_shape=jax.ShapeDtypeStruct(
            (key_devices, bucket_rows + extra_rows, fact_width + out_width), bf16
        ),
        in_specs=[pl.BlockSpec(memory_space=pl.ANY)] * 4,
        out_specs=pl.BlockSpec(memory_space=pltpu.VMEM),
        scratch_shapes=[
            pltpu.VMEM((key_devices, bucket_rows), i32),
            pltpu.SMEM((1, key_devices), i32),
            pltpu.SemaphoreType.DMA((4,)),
        ],
    )(
        fact_keys.reshape(key_devices, bucket_rows),
        fill_counts,
        fact_features.reshape(key_devices, bucket_rows, fact_width),
        targets.reshape(key_devices, bucket_rows, out_width),
    )
    packed = spread(packed, "key")
    rows = lax.all_gather(dim_features, "fact", axis=0, tiled=True, axis_index_groups=one_y)

    met = kernel_call(
        sum_by_key,
        (ring_size, ring_keys + extra_rows, 2 * out_width),
        bf16,
        packed,
        fact_weight,
        rows,
        dim_weight,
    )
    met = spread(met, "fact", one_z)
    terms = kernel_call(
        both_terms, (fact_width + dim_width, out_width), f32, packed, fact_weight, rows, met
    )

    totals = total_over_devices(terms, one_y, chip, plane)
    total_rows = slot_count * fact_devices * key_devices
    row_scale = float(total_rows) ** (-0.5)
    vmem = pl.BlockSpec(memory_space=pltpu.VMEM)
    return tuple(
        pl.pallas_call(
            functools.partial(finish, row_scale),
            out_shape=(
                jax.ShapeDtypeStruct((fact_width, out_width), f32),
                jax.ShapeDtypeStruct((dim_width, out_width), f32),
            ),
            in_specs=[vmem] * 3,
            out_specs=(vmem, vmem),
            compiler_params=pltpu.CompilerParams(vmem_limit_bytes=16 << 20),
        )(totals, fact_weight, dim_weight)
    )


def solution(mesh):
    placed = (
        P(("fact", "key"), None),
        P(("fact", "key"), None),
        P(("fact", "key")),
        P(("fact", "key"), None),
        P(("fact", "key"), None),
        P(),
        P(),
    )
    return jax.shard_map(
        on_device, mesh=mesh, in_specs=placed, out_specs=(P(), P()), check_vma=False
    )
```

```python
import functools

import jax
import jax.numpy as jnp
from jax import lax
from jax.experimental import pallas as pl
from jax.experimental.pallas import tpu as pltpu
from jax.sharding import PartitionSpec as P

ridge_weight = 4.0
ring_size = 8
digit = 64
extra_rows = 8
f32, bf16, i32 = jnp.float32, jnp.bfloat16, jnp.int32


def groups_of(fact_devices, key_devices):
    levels = range(fact_devices // ring_size)
    chips, cores = range(key_devices // 2), range(2)
    one_z = [[z * ring_size + y for y in range(ring_size)] for z in levels]
    one_y = [[z * ring_size + y for z in levels] for y in range(ring_size)]
    chip = [[2 * x + core for core in cores] for x in chips]
    plane = [
        [(z * ring_size + y) * key_devices + 2 * x + core for y in range(ring_size) for x in chips]
        for z in levels
        for core in cores
    ]
    return one_z, one_y, chip, plane


def spread(array, axis, groups=None):
    return lax.all_to_all(
        array, axis, split_axis=0, concat_axis=0, tiled=True, axis_index_groups=groups
    )


def collect(array, axis, copies, groups):
    return spread(jnp.broadcast_to(array[None], (copies, *array.shape)), axis, groups)


def total_over_devices(kept, given, one_y, chip, plane):
    rows, width = kept.shape
    both = ("fact", "key")
    members = len(plane[0])
    swap = [(a, b) for pair in chip for a, b in (pair, pair[::-1])]
    part = kept + lax.ppermute(given, "key", swap)
    part = spread(part.reshape(members, -1, 4, width), both, plane).sum(axis=0)
    part = collect(part, "fact", len(one_y[0]), one_y).sum(axis=0)
    part = collect(part, both, members, plane).reshape(-1, 4, width)
    part = lax.all_gather(part, "key", axis=0, tiled=True, axis_index_groups=chip)
    return part.reshape(2 * rows, width)


def pack_slots(
    own_keys, ring_keys, keys_hbm, fill_hbm, features_hbm, targets_hbm, out_ref, keys_ref, fill_ref, done
):
    buckets, bucket_rows, width = features_hbm.shape
    out_width = targets_hbm.shape[2]
    slots = pl.ds(0, bucket_rows)
    copies = [
        pltpu.make_async_copy(keys_hbm, keys_ref, done.at[0]),
        pltpu.make_async_copy(fill_hbm, fill_ref, done.at[1]),
        pltpu.make_async_copy(features_hbm, out_ref.at[:, slots, pl.ds(0, width)], done.at[2]),
        pltpu.make_async_copy(targets_hbm, out_ref.at[:, slots, pl.ds(width, out_width)], done.at[3]),
    ]
    for copy in copies:
        copy.start()
    copies[0].wait()
    copies[1].wait()
    keys = keys_ref[...]
    owner = keys // (own_keys * buckets)
    places = (owner % ring_size) * ring_keys + (owner // ring_size) * own_keys + keys % own_keys
    slot = lax.broadcasted_iota(i32, (1, bucket_rows), 1)
    for b in range(buckets):
        codes = jnp.where(slot < fill_ref[0, b], places[b : b + 1], -digit)
        high = codes // digit
        low = codes - high * digit
        digits = jnp.concatenate([high, low, jnp.zeros_like(high)], axis=1).astype(f32)
        digits = jnp.broadcast_to(digits, (extra_rows, width + out_width))
        out_ref[b, pl.ds(bucket_rows, extra_rows), :] = digits.astype(bf16)
    for copy in copies[2:]:
        copy.wait()


def codes_of(packed_ref, b):
    bucket_rows = packed_ref.shape[1] - extra_rows
    digits = packed_ref[b, pl.ds(bucket_rows, extra_rows), :].astype(f32)
    codes = digits[:, :bucket_rows] * digit + digits[:, bucket_rows : 2 * bucket_rows]
    return codes.astype(i32)[:1]


def partial_of(packed_ref, weight_ref, pair):
    slots = pl.ds(0, packed_ref.shape[1] - extra_rows)
    width = weight_ref.shape[0]
    rows = jnp.concatenate([packed_ref[b, slots, :] for b in pair], axis=0)
    features = rows[:, :width]
    value = jnp.dot(features, weight_ref[...], preferred_element_type=f32)
    return features, value - rows[:, width:].astype(f32)


def pairs_of(packed_ref):
    return [(b, b + 1) for b in range(0, packed_ref.shape[0], 2)]


def diagonal_of(rows, columns):
    return lax.broadcasted_iota(i32, (rows, columns), 0) == lax.broadcasted_iota(
        i32, (rows, columns), 1
    )


def sum_by_key(packed_ref, weight_ref, rows_ref, dim_weight_ref, out_ref):
    members, _, two_widths = out_ref.shape
    out_width = two_widths // 2
    ring_keys = rows_ref.shape[0]
    two_rows = 2 * (packed_ref.shape[1] - extra_rows)
    places = lax.broadcasted_iota(i32, (members * ring_keys, two_rows), 0)
    ones = jnp.ones((two_rows, out_width), bf16)
    sums = jnp.zeros((members * ring_keys, two_widths), f32)
    for pair in pairs_of(packed_ref):
        codes = jnp.concatenate([codes_of(packed_ref, b) for b in pair], axis=1)
        one_hot = jnp.where(places == codes, f32(1.0), f32(0.0)).astype(bf16)
        _, value = partial_of(packed_ref, weight_ref, pair)
        value = jnp.concatenate([value.astype(bf16), ones], axis=1)
        sums += jnp.dot(one_hot, value, preferred_element_type=f32)
    values = jnp.dot(rows_ref[...], dim_weight_ref[...], preferred_element_type=f32).astype(bf16)
    diagonal = diagonal_of(ring_keys, out_width)
    own = pl.ds(0, ring_keys)
    for m in range(members):
        part = sums[m * ring_keys : (m + 1) * ring_keys]
        out_ref[m, own, pl.ds(0, out_width)] = part[:, :out_width].astype(bf16)
        out_ref[m, own, pl.ds(out_width, out_width)] = values
        counts = jnp.where(diagonal, part[:, out_width:], f32(0.0)).sum(axis=0, keepdims=True)
        high = jnp.floor(counts * (1.0 / digit))
        digits = jnp.concatenate([high, counts - high * digit], axis=1)
        digits = jnp.broadcast_to(digits, (extra_rows, two_widths))
        out_ref[m, pl.ds(ring_keys, extra_rows), :] = digits.astype(bf16)


def both_terms(packed_ref, weight_ref, rows_ref, met_ref, kept_ref, given_ref):
    members, _, two_widths = met_ref.shape
    out_width = two_widths // 2
    ring_keys = rows_ref.shape[0]
    buckets = packed_ref.shape[0]
    bucket_rows = packed_ref.shape[1] - extra_rows
    width = weight_ref.shape[0]
    contract = (((0,), (0,)), ((), ()))

    own = pl.ds(0, ring_keys)
    values = jnp.concatenate(
        [met_ref[m, own, pl.ds(out_width, out_width)] for m in range(members)], axis=0
    )
    codes = jnp.concatenate([codes_of(packed_ref, b) for b in range(buckets)], axis=0)
    codes = jnp.transpose(codes.astype(f32)).astype(i32)
    places = lax.broadcasted_iota(i32, (bucket_rows, members * ring_keys), 1)
    fact_term = jnp.zeros((width, out_width), f32)
    for pair in pairs_of(packed_ref):
        one_hot = [
            jnp.where(places == codes[:, b : b + 1], f32(1.0), f32(0.0)).astype(bf16) for b in pair
        ]
        features, value = partial_of(packed_ref, weight_ref, pair)
        found = jnp.dot(jnp.concatenate(one_hot, axis=0), values, preferred_element_type=f32)
        live = jnp.concatenate([codes[:, b : b + 1] for b in pair], axis=0) >= 0
        residual = jnp.where(live, value + found, f32(0.0)).astype(bf16)
        fact_term += lax.dot_general(features, residual, contract, preferred_element_type=f32)
    me = lax.rem(lax.axis_index("fact"), ring_size)
    sums = jnp.zeros((ring_keys, out_width), f32)
    digits = jnp.zeros((extra_rows, two_widths), f32)
    for m in range(members):
        sums += met_ref[m, own, pl.ds(0, out_width)].astype(f32)
        digits += met_ref[m, pl.ds(ring_keys, extra_rows), :].astype(f32)
    counts = digits[:1, :out_width] * digit + digits[:1, out_width:]
    diagonal = diagonal_of(ring_keys, out_width)
    counts = jnp.sum(jnp.where(diagonal, counts, f32(0.0)), axis=1, keepdims=True)
    sums += counts * met_ref[me, own, pl.ds(out_width, out_width)].astype(f32)
    high = sums.astype(bf16)
    low = (sums - high.astype(f32)).astype(bf16)
    dim_term = lax.dot_general(
        rows_ref[...], jnp.concatenate([high, low], axis=1), contract, preferred_element_type=f32
    )
    dim_term = dim_term[:, :out_width] + dim_term[:, out_width:]
    half = kept_ref.shape[0]

    def store(upper_ref, lower_ref):
        upper_ref[pl.ds(0, width), :] = fact_term
        upper_ref[pl.ds(width, half - width), :] = dim_term[: half - width]
        lower_ref[...] = dim_term[half - width :]

    core = lax.rem(lax.axis_index("key"), 2)
    pl.when(core == 0)(lambda: store(kept_ref, given_ref))
    pl.when(core == 1)(lambda: store(given_ref, kept_ref))


def finish(row_scale, totals_ref, fact_weight_ref, dim_weight_ref, fact_ref, dim_ref):
    width = fact_ref.shape[0]
    fact_ref[...] = totals_ref[pl.ds(0, width), :] * row_scale + ridge_weight * fact_weight_ref[
        ...
    ].astype(f32)
    dim_ref[...] = totals_ref[
        pl.ds(width, dim_ref.shape[0]), :
    ] * row_scale + ridge_weight * dim_weight_ref[...].astype(f32)


def kernel_call(body, shapes, dtype, *operands):
    vmem = pl.BlockSpec(memory_space=pltpu.VMEM)
    return pl.pallas_call(
        body,
        out_shape=tuple(jax.ShapeDtypeStruct(shape, dtype) for shape in shapes),
        in_specs=[vmem] * len(operands),
        out_specs=(vmem,) * len(shapes),
        compiler_params=pltpu.CompilerParams(vmem_limit_bytes=32 << 20),
    )(*operands)


def on_device(
    fact_features, targets, fact_keys, fill_counts, dim_features, fact_weight, dim_weight
):
    key_devices = lax.axis_size("key")
    fact_devices = lax.axis_size("fact")
    one_z, one_y, chip, plane = groups_of(fact_devices, key_devices)
    slot_count = fact_keys.shape[0]
    bucket_rows = slot_count // key_devices
    own_keys, dim_width = dim_features.shape
    fact_width, out_width = fact_weight.shape
    ring_keys = len(one_z) * own_keys

    packed = pl.pallas_call(
        functools.partial(pack_slots, own_keys, ring_keys),
        out_shape=jax.ShapeDtypeStruct(
            (key_devices, bucket_rows + extra_rows, fact_width + out_width), bf16
        ),
        in_specs=[pl.BlockSpec(memory_space=pl.ANY)] * 4,
        out_specs=pl.BlockSpec(memory_space=pltpu.VMEM),
        scratch_shapes=[
            pltpu.VMEM((key_devices, bucket_rows), i32),
            pltpu.SMEM((1, key_devices), i32),
            pltpu.SemaphoreType.DMA((4,)),
        ],
    )(
        fact_keys.reshape(key_devices, bucket_rows),
        fill_counts,
        fact_features.reshape(key_devices, bucket_rows, fact_width),
        targets.reshape(key_devices, bucket_rows, out_width),
    )
    packed = spread(packed, "key")
    rows = lax.all_gather(dim_features, "fact", axis=0, tiled=True, axis_index_groups=one_y)

    (met,) = kernel_call(
        sum_by_key,
        ((ring_size, ring_keys + extra_rows, 2 * out_width),),
        bf16,
        packed,
        fact_weight,
        rows,
        dim_weight,
    )
    met = spread(met, "fact", one_z)
    half = ((fact_width + dim_width) // 2, out_width)
    kept, given = kernel_call(both_terms, (half, half), f32, packed, fact_weight, rows, met)
    totals = total_over_devices(kept, given, one_y, chip, plane)
    total_rows = slot_count * fact_devices * key_devices
    row_scale = float(total_rows) ** (-0.5)
    vmem = pl.BlockSpec(memory_space=pltpu.VMEM)
    return tuple(
        pl.pallas_call(
            functools.partial(finish, row_scale),
            out_shape=(
                jax.ShapeDtypeStruct((fact_width, out_width), f32),
                jax.ShapeDtypeStruct((dim_width, out_width), f32),
            ),
            in_specs=[vmem] * 3,
            out_specs=(vmem, vmem),
            compiler_params=pltpu.CompilerParams(vmem_limit_bytes=16 << 20),
        )(totals, fact_weight, dim_weight)
    )


def solution(mesh):
    placed = (
        P(("fact", "key"), None),
        P(("fact", "key"), None),
        P(("fact", "key")),
        P(("fact", "key"), None),
        P(("fact", "key"), None),
        P(),
        P(),
    )
    return jax.shard_map(
        on_device, mesh=mesh, in_specs=placed, out_specs=(P(), P()), check_vma=False
    )
```

```python
import functools

import jax
import jax.numpy as jnp
from jax import lax
from jax.experimental import pallas as pl
from jax.experimental.pallas import tpu as pltpu
from jax.sharding import PartitionSpec as P

ridge_weight = 4.0
ring_size = 8
digit = 64
extra_rows = 8
f32, bf16, i32 = jnp.float32, jnp.bfloat16, jnp.int32


def groups_of(fact_devices, key_devices):
    levels = range(fact_devices // ring_size)
    chips, cores = range(key_devices // 2), range(2)
    one_z = [[z * ring_size + y for y in range(ring_size)] for z in levels]
    one_y = [[z * ring_size + y for z in levels] for y in range(ring_size)]
    chip = [[2 * x + core for core in cores] for x in chips]
    plane = [
        [(z * ring_size + y) * key_devices + 2 * x + core for y in range(ring_size) for x in chips]
        for z in levels
        for core in cores
    ]
    return one_z, one_y, chip, plane


def spread(array, axis, groups=None):
    return lax.all_to_all(
        array, axis, split_axis=0, concat_axis=0, tiled=True, axis_index_groups=groups
    )


def collect(array, axis, copies, groups):
    return spread(jnp.broadcast_to(array[None], (copies, *array.shape)), axis, groups)


def total_over_devices(kept, given, one_y, chip, plane):
    rows, width = kept.shape
    both = ("fact", "key")
    members = len(plane[0])
    swap = [(a, b) for pair in chip for a, b in (pair, pair[::-1])]
    part = kept + lax.ppermute(given, "key", swap)
    part = spread(part.reshape(members, -1, 4, width), both, plane).sum(axis=0)
    part = collect(part, "fact", len(one_y[0]), one_y).sum(axis=0)
    part = collect(part, both, members, plane).reshape(-1, 4, width)
    part = lax.all_gather(part, "key", axis=0, tiled=True, axis_index_groups=chip)
    return part.reshape(2 * rows, width)


def pack_slots(
    own_keys, ring_keys, keys_hbm, fill_hbm, features_hbm, targets_hbm, out_hbm, keys_ref, fill_ref, slots_ref, done
):
    buckets, bucket_rows, width = features_hbm.shape
    out_width = targets_hbm.shape[2]
    slots = pl.ds(0, bucket_rows)
    groups = range(buckets // 2)

    def copies(g):
        two = pl.ds(2 * g, 2)
        return (
            pltpu.make_async_copy(
                features_hbm.at[two], slots_ref.at[two, slots, pl.ds(0, width)], done.at[g, 0]
            ),
            pltpu.make_async_copy(
                targets_hbm.at[two], slots_ref.at[two, slots, pl.ds(width, out_width)], done.at[g, 1]
            ),
            pltpu.make_async_copy(slots_ref.at[two], out_hbm.at[two], done.at[g, 2]),
        )

    keys_in = pltpu.make_async_copy(keys_hbm, keys_ref, done.at[len(groups), 0])
    fill_in = pltpu.make_async_copy(fill_hbm, fill_ref, done.at[len(groups), 1])
    keys_in.start()
    fill_in.start()
    for g in groups:
        for copy in copies(g)[:2]:
            copy.start()
    keys_in.wait()
    fill_in.wait()
    keys = keys_ref[...]
    owner = keys // (own_keys * buckets)
    places = (owner % ring_size) * ring_keys + (owner // ring_size) * own_keys + keys % own_keys
    slot = lax.broadcasted_iota(i32, (1, bucket_rows), 1)
    for b in range(buckets):
        codes = jnp.where(slot < fill_ref[0, b], places[b : b + 1], -digit)
        high = codes // digit
        low = codes - high * digit
        digits = jnp.concatenate([high, low, jnp.zeros_like(high)], axis=1).astype(f32)
        digits = jnp.broadcast_to(digits, (extra_rows, width + out_width))
        slots_ref[b, pl.ds(bucket_rows, extra_rows), :] = digits.astype(bf16)
    for g in groups:
        features_in, targets_in, out = copies(g)
        features_in.wait()
        targets_in.wait()
        out.start()
    for g in groups:
        copies(g)[2].wait()


def codes_of(packed_ref, b):
    bucket_rows = packed_ref.shape[1] - extra_rows
    digits = packed_ref[b, pl.ds(bucket_rows, extra_rows), :].astype(f32)
    codes = digits[:, :bucket_rows] * digit + digits[:, bucket_rows : 2 * bucket_rows]
    return codes.astype(i32)[:1]


def partial_of(packed_ref, weight_ref, pair):
    slots = pl.ds(0, packed_ref.shape[1] - extra_rows)
    width = weight_ref.shape[0]
    rows = jnp.concatenate([packed_ref[b, slots, :] for b in pair], axis=0)
    features = rows[:, :width]
    value = jnp.dot(features, weight_ref[...], preferred_element_type=f32)
    return features, value - rows[:, width:].astype(f32)


def pairs_of(packed_ref):
    return [(b, b + 1) for b in range(0, packed_ref.shape[0], 2)]


def diagonal_of(rows, columns):
    return lax.broadcasted_iota(i32, (rows, columns), 0) == lax.broadcasted_iota(
        i32, (rows, columns), 1
    )


def sum_by_key(packed_ref, weight_ref, rows_ref, dim_weight_ref, out_ref):
    members, _, two_widths = out_ref.shape
    out_width = two_widths // 2
    ring_keys = rows_ref.shape[0]
    two_rows = 2 * (packed_ref.shape[1] - extra_rows)
    places = lax.broadcasted_iota(i32, (members * ring_keys, two_rows), 0)
    ones = jnp.ones((two_rows, out_width), bf16)
    sums = jnp.zeros((members * ring_keys, two_widths), f32)
    for pair in pairs_of(packed_ref):
        codes = jnp.concatenate([codes_of(packed_ref, b) for b in pair], axis=1)
        one_hot = jnp.where(places == codes, f32(1.0), f32(0.0)).astype(bf16)
        _, value = partial_of(packed_ref, weight_ref, pair)
        value = jnp.concatenate([value.astype(bf16), ones], axis=1)
        sums += jnp.dot(one_hot, value, preferred_element_type=f32)
    values = jnp.dot(rows_ref[...], dim_weight_ref[...], preferred_element_type=f32).astype(bf16)
    diagonal = diagonal_of(ring_keys, out_width)
    own = pl.ds(0, ring_keys)
    for m in range(members):
        part = sums[m * ring_keys : (m + 1) * ring_keys]
        out_ref[m, own, pl.ds(0, out_width)] = part[:, :out_width].astype(bf16)
        out_ref[m, own, pl.ds(out_width, out_width)] = values
        counts = jnp.where(diagonal, part[:, out_width:], f32(0.0)).sum(axis=0, keepdims=True)
        high = jnp.floor(counts * (1.0 / digit))
        digits = jnp.concatenate([high, counts - high * digit], axis=1)
        digits = jnp.broadcast_to(digits, (extra_rows, two_widths))
        out_ref[m, pl.ds(ring_keys, extra_rows), :] = digits.astype(bf16)


def both_terms(packed_ref, weight_ref, rows_ref, met_ref, kept_ref, given_ref):
    members, _, two_widths = met_ref.shape
    out_width = two_widths // 2
    ring_keys = rows_ref.shape[0]
    buckets = packed_ref.shape[0]
    bucket_rows = packed_ref.shape[1] - extra_rows
    width = weight_ref.shape[0]
    contract = (((0,), (0,)), ((), ()))

    own = pl.ds(0, ring_keys)
    values = jnp.concatenate(
        [met_ref[m, own, pl.ds(out_width, out_width)] for m in range(members)], axis=0
    )
    codes = jnp.concatenate([codes_of(packed_ref, b) for b in range(buckets)], axis=0)
    codes = jnp.transpose(codes.astype(f32)).astype(i32)
    places = lax.broadcasted_iota(i32, (bucket_rows, members * ring_keys), 1)
    fact_term = jnp.zeros((width, out_width), f32)
    for pair in pairs_of(packed_ref):
        one_hot = [
            jnp.where(places == codes[:, b : b + 1], f32(1.0), f32(0.0)).astype(bf16) for b in pair
        ]
        features, value = partial_of(packed_ref, weight_ref, pair)
        found = jnp.dot(jnp.concatenate(one_hot, axis=0), values, preferred_element_type=f32)
        live = jnp.concatenate([codes[:, b : b + 1] for b in pair], axis=0) >= 0
        residual = jnp.where(live, value + found, f32(0.0)).astype(bf16)
        fact_term += lax.dot_general(features, residual, contract, preferred_element_type=f32)
    me = lax.rem(lax.axis_index("fact"), ring_size)
    sums = jnp.zeros((ring_keys, out_width), f32)
    digits = jnp.zeros((extra_rows, two_widths), f32)
    for m in range(members):
        sums += met_ref[m, own, pl.ds(0, out_width)].astype(f32)
        digits += met_ref[m, pl.ds(ring_keys, extra_rows), :].astype(f32)
    counts = digits[:1, :out_width] * digit + digits[:1, out_width:]
    diagonal = diagonal_of(ring_keys, out_width)
    counts = jnp.sum(jnp.where(diagonal, counts, f32(0.0)), axis=1, keepdims=True)
    sums += counts * met_ref[me, own, pl.ds(out_width, out_width)].astype(f32)
    high = sums.astype(bf16)
    low = (sums - high.astype(f32)).astype(bf16)
    dim_term = lax.dot_general(
        rows_ref[...], jnp.concatenate([high, low], axis=1), contract, preferred_element_type=f32
    )
    dim_term = dim_term[:, :out_width] + dim_term[:, out_width:]
    half = kept_ref.shape[0]

    def store(upper_ref, lower_ref):
        upper_ref[pl.ds(0, width), :] = fact_term
        upper_ref[pl.ds(width, half - width), :] = dim_term[: half - width]
        lower_ref[...] = dim_term[half - width :]

    core = lax.rem(lax.axis_index("key"), 2)
    pl.when(core == 0)(lambda: store(kept_ref, given_ref))
    pl.when(core == 1)(lambda: store(given_ref, kept_ref))


def finish(row_scale, totals_ref, fact_weight_ref, dim_weight_ref, fact_ref, dim_ref):
    width = fact_ref.shape[0]
    fact_ref[...] = totals_ref[pl.ds(0, width), :] * row_scale + ridge_weight * fact_weight_ref[
        ...
    ].astype(f32)
    dim_ref[...] = totals_ref[
        pl.ds(width, dim_ref.shape[0]), :
    ] * row_scale + ridge_weight * dim_weight_ref[...].astype(f32)


def kernel_call(body, shapes, dtype, *operands):
    vmem = pl.BlockSpec(memory_space=pltpu.VMEM)
    return pl.pallas_call(
        body,
        out_shape=tuple(jax.ShapeDtypeStruct(shape, dtype) for shape in shapes),
        in_specs=[vmem] * len(operands),
        out_specs=(vmem,) * len(shapes),
        compiler_params=pltpu.CompilerParams(vmem_limit_bytes=32 << 20),
    )(*operands)


def on_device(
    fact_features, targets, fact_keys, fill_counts, dim_features, fact_weight, dim_weight
):
    key_devices = lax.axis_size("key")
    fact_devices = lax.axis_size("fact")
    one_z, one_y, chip, plane = groups_of(fact_devices, key_devices)
    slot_count = fact_keys.shape[0]
    bucket_rows = slot_count // key_devices
    own_keys, dim_width = dim_features.shape
    fact_width, out_width = fact_weight.shape
    ring_keys = len(one_z) * own_keys

    packed = pl.pallas_call(
        functools.partial(pack_slots, own_keys, ring_keys),
        out_shape=jax.ShapeDtypeStruct(
            (key_devices, bucket_rows + extra_rows, fact_width + out_width), bf16
        ),
        in_specs=[pl.BlockSpec(memory_space=pl.ANY)] * 4,
        out_specs=pl.BlockSpec(memory_space=pl.ANY),
        scratch_shapes=[
            pltpu.VMEM((key_devices, bucket_rows), i32),
            pltpu.SMEM((1, key_devices), i32),
            pltpu.VMEM((key_devices, bucket_rows + extra_rows, fact_width + out_width), bf16),
            pltpu.SemaphoreType.DMA((key_devices // 2 + 1, 3)),
        ],
    )(
        fact_keys.reshape(key_devices, bucket_rows),
        fill_counts,
        fact_features.reshape(key_devices, bucket_rows, fact_width),
        targets.reshape(key_devices, bucket_rows, out_width),
    )
    packed = spread(packed, "key")
    rows = lax.all_gather(dim_features, "fact", axis=0, tiled=True, axis_index_groups=one_y)

    (met,) = kernel_call(
        sum_by_key,
        ((ring_size, ring_keys + extra_rows, 2 * out_width),),
        bf16,
        packed,
        fact_weight,
        rows,
        dim_weight,
    )
    met = spread(met, "fact", one_z)
    half = ((fact_width + dim_width) // 2, out_width)
    kept, given = kernel_call(both_terms, (half, half), f32, packed, fact_weight, rows, met)
    totals = total_over_devices(kept, given, one_y, chip, plane)
    total_rows = slot_count * fact_devices * key_devices
    row_scale = float(total_rows) ** (-0.5)
    vmem = pl.BlockSpec(memory_space=pltpu.VMEM)
    return tuple(
        pl.pallas_call(
            functools.partial(finish, row_scale),
            out_shape=(
                jax.ShapeDtypeStruct((fact_width, out_width), f32),
                jax.ShapeDtypeStruct((dim_width, out_width), f32),
            ),
            in_specs=[vmem] * 3,
            out_specs=(vmem, vmem),
            compiler_params=pltpu.CompilerParams(vmem_limit_bytes=16 << 20),
        )(totals, fact_weight, dim_weight)
    )


def solution(mesh):
    placed = (
        P(("fact", "key"), None),
        P(("fact", "key"), None),
        P(("fact", "key")),
        P(("fact", "key"), None),
        P(("fact", "key"), None),
        P(),
        P(),
    )
    return jax.shard_map(
        on_device, mesh=mesh, in_specs=placed, out_specs=(P(), P()), check_vma=False
    )
```

```python
import functools

import jax
import jax.numpy as jnp
from jax import lax
from jax.experimental import pallas as pl
from jax.experimental.pallas import tpu as pltpu
from jax.sharding import PartitionSpec as P

ridge_weight = 4.0
ring_size = 8
digit = 64
extra_rows = 8
f32, bf16, i32 = jnp.float32, jnp.bfloat16, jnp.int32


def groups_of(fact_devices, key_devices):
    levels = range(fact_devices // ring_size)
    chips, cores = range(key_devices // 2), range(2)
    one_z = [[z * ring_size + y for y in range(ring_size)] for z in levels]
    one_y = [[z * ring_size + y for z in levels] for y in range(ring_size)]
    near = [line[i : i + 3] for line in one_y for i in range(0, len(line), 3)]
    far = [line[i::3] for line in one_y for i in range(3)]
    chip = [[2 * x + core for core in cores] for x in chips]
    plane = [
        [(z * ring_size + y) * key_devices + 2 * x + core for y in range(ring_size) for x in chips]
        for z in levels
        for core in cores
    ]
    return one_z, one_y, near, far, chip, plane


def spread(array, axis, groups=None):
    return lax.all_to_all(
        array, axis, split_axis=0, concat_axis=0, tiled=True, axis_index_groups=groups
    )


def collect(array, axis, copies, groups):
    return spread(jnp.broadcast_to(array[None], (copies, *array.shape)), axis, groups)


def total_over_devices(kept, given, one_y, chip, plane):
    rows, width = kept.shape
    both = ("fact", "key")
    members = len(plane[0])
    swap = [(a, b) for pair in chip for a, b in (pair, pair[::-1])]
    part = kept + lax.ppermute(given, "key", swap)
    part = spread(part.reshape(members, -1, 4, width), both, plane).sum(axis=0)
    part = collect(part, "fact", len(one_y[0]), one_y).sum(axis=0)
    part = collect(part, both, members, plane).reshape(-1, 4, width)
    part = lax.all_gather(part, "key", axis=0, tiled=True, axis_index_groups=chip)
    return part.reshape(2 * rows, width)


def pack_slots(
    own_keys, ring_keys, keys_hbm, fill_hbm, features_hbm, targets_hbm, out_hbm, keys_ref, fill_ref, slots_ref, done
):
    buckets, bucket_rows, width = features_hbm.shape
    out_width = targets_hbm.shape[2]
    slots = pl.ds(0, bucket_rows)
    groups = range(buckets // 2)

    def copies(g):
        two = pl.ds(2 * g, 2)
        return (
            pltpu.make_async_copy(
                features_hbm.at[two], slots_ref.at[two, slots, pl.ds(0, width)], done.at[g, 0]
            ),
            pltpu.make_async_copy(
                targets_hbm.at[two], slots_ref.at[two, slots, pl.ds(width, out_width)], done.at[g, 1]
            ),
            pltpu.make_async_copy(slots_ref.at[two], out_hbm.at[two], done.at[g, 2]),
        )

    keys_in = pltpu.make_async_copy(keys_hbm, keys_ref, done.at[len(groups), 0])
    fill_in = pltpu.make_async_copy(fill_hbm, fill_ref, done.at[len(groups), 1])
    keys_in.start()
    fill_in.start()
    plan = [copies(g) for g in groups]
    for features_in, targets_in, _ in plan:
        features_in.start()
        targets_in.start()
    keys_in.wait()
    fill_in.wait()
    keys = keys_ref[...]
    owner = keys // (own_keys * buckets)
    places = (owner % ring_size) * ring_keys + (owner // ring_size) * own_keys + keys % own_keys
    slot = lax.broadcasted_iota(i32, (1, bucket_rows), 1)
    for b in range(buckets):
        codes = jnp.where(slot < fill_ref[0, b], places[b : b + 1], -digit)
        high = codes // digit
        low = codes - high * digit
        digits = jnp.concatenate([high, low, jnp.zeros_like(high)], axis=1).astype(f32)
        digits = jnp.broadcast_to(digits, (extra_rows, width + out_width))
        slots_ref[b, pl.ds(bucket_rows, extra_rows), :] = digits.astype(bf16)
    for features_in, targets_in, out in plan:
        features_in.wait()
        targets_in.wait()
        out.start()
    for _, _, out in plan:
        out.wait()


def codes_of(packed_ref, b):
    bucket_rows = packed_ref.shape[1] - extra_rows
    digits = packed_ref[b, pl.ds(bucket_rows, extra_rows), :].astype(f32)
    codes = digits[:, :bucket_rows] * digit + digits[:, bucket_rows : 2 * bucket_rows]
    return codes.astype(i32)[:1]


def partial_of(packed_ref, weight_ref, pair):
    slots = pl.ds(0, packed_ref.shape[1] - extra_rows)
    width = weight_ref.shape[0]
    rows = jnp.concatenate([packed_ref[b, slots, :] for b in pair], axis=0)
    features = rows[:, :width]
    value = jnp.dot(features, weight_ref[...], preferred_element_type=f32)
    return features, value - rows[:, width:].astype(f32)


def pairs_of(packed_ref):
    return [(b, b + 1) for b in range(0, packed_ref.shape[0], 2)]


def diagonal_of(rows, columns):
    return lax.broadcasted_iota(i32, (rows, columns), 0) == lax.broadcasted_iota(
        i32, (rows, columns), 1
    )


def split(value):
    high = value.astype(bf16)
    return high, (value - high.astype(f32)).astype(bf16)


contract = (((0,), (0,)), ((), ()))


def own_term(packed_ref, weight_ref, out_ref):
    out_width = weight_ref.shape[1]
    codes = [codes_of(packed_ref, b) for b in range(packed_ref.shape[0])]
    codes = jnp.transpose(jnp.concatenate(codes, axis=0).astype(f32))
    total = jnp.zeros((weight_ref.shape[0], 2 * out_width), f32)
    for pair in pairs_of(packed_ref):
        features, value = partial_of(packed_ref, weight_ref, pair)
        live = jnp.concatenate([codes[:, b : b + 1] for b in pair], axis=0) >= 0.0
        value = jnp.concatenate(split(jnp.where(live, value, f32(0.0))), axis=1)
        total += lax.dot_general(features, value, contract, preferred_element_type=f32)
    out_ref[...] = total[:, :out_width] + total[:, out_width:]


def sum_by_key(packed_ref, rows_ref, own_ref, out_ref, rows_out_ref, own_out_ref):
    members, _, width = out_ref.shape
    ring_keys = out_ref.shape[1] - extra_rows
    bucket_rows = packed_ref.shape[1] - extra_rows
    slots = pl.ds(0, bucket_rows)
    places = lax.broadcasted_iota(i32, (members * ring_keys, 2 * bucket_rows), 0)
    ones = jnp.ones((2 * bucket_rows, 128), bf16)
    sums = jnp.zeros((members * ring_keys, width + 128), f32)
    for pair in pairs_of(packed_ref):
        codes = jnp.concatenate([codes_of(packed_ref, b) for b in pair], axis=1)
        one_hot = jnp.where(places == codes, f32(1.0), f32(0.0)).astype(bf16)
        value = jnp.concatenate([packed_ref[b, slots, :] for b in pair], axis=0)
        value = jnp.concatenate([value, ones], axis=1)
        sums += jnp.dot(one_hot, value, preferred_element_type=f32)
    diagonal = diagonal_of(ring_keys, 128)
    for m in range(members):
        part = sums[m * ring_keys : (m + 1) * ring_keys]
        out_ref[m, pl.ds(0, ring_keys), :] = part[:, :width].astype(bf16)
        counts = jnp.where(diagonal, part[:, width:], f32(0.0)).sum(axis=0, keepdims=True)
        high = jnp.floor(counts * (1.0 / digit))
        rest = jnp.zeros((1, width - 256), f32)
        digits = jnp.concatenate([high, counts - high * digit, rest], axis=1)
        out_ref[m, pl.ds(ring_keys, extra_rows), :] = jnp.broadcast_to(
            digits, (extra_rows, width)
        ).astype(bf16)
    rows_out_ref[...] = rows_ref[...]
    own_out_ref[...] = own_ref[...]


def both_terms(own_ref, weight_ref, rows_ref, dim_weight_ref, met_ref, kept_ref, given_ref):
    members = met_ref.shape[0]
    ring_keys, dim_width = rows_ref.shape
    width, out_width = weight_ref.shape
    keys = pl.ds(0, ring_keys)
    rows = rows_ref[...]
    values = jnp.dot(rows, dim_weight_ref[...], preferred_element_type=f32).astype(bf16)
    met = jnp.zeros((ring_keys, width + out_width), f32)
    digits = jnp.zeros((extra_rows, width + out_width), f32)
    for m in range(members):
        met += met_ref[m, keys, :].astype(f32)
        digits += met_ref[m, pl.ds(ring_keys, extra_rows), :].astype(f32)
    counts = digits[:1, :128] * digit + digits[:1, 128:256]
    diagonal = diagonal_of(ring_keys, 128)
    counts = jnp.sum(jnp.where(diagonal, counts, f32(0.0)), axis=1, keepdims=True)
    high, low = split(met[:, :width])
    sums = jnp.dot(high, weight_ref[...], preferred_element_type=f32)
    sums += jnp.dot(low, weight_ref[...], preferred_element_type=f32)
    sums += counts * values.astype(f32) - met[:, width:]
    fact_term = own_ref[...]
    fact_term += lax.dot_general(high, values, contract, preferred_element_type=f32)
    fact_term += lax.dot_general(low, values, contract, preferred_element_type=f32)
    sums = jnp.concatenate(split(sums), axis=1)
    dim_term = lax.dot_general(rows, sums, contract, preferred_element_type=f32)
    dim_term = dim_term[:, :out_width] + dim_term[:, out_width:]
    half = kept_ref.shape[0]

    def store(upper_ref, lower_ref):
        upper_ref[pl.ds(0, width), :] = fact_term
        upper_ref[pl.ds(width, half - width), :] = dim_term[: half - width]
        lower_ref[...] = dim_term[half - width :]

    core = lax.rem(lax.axis_index("key"), 2)
    pl.when(core == 0)(lambda: store(kept_ref, given_ref))
    pl.when(core == 1)(lambda: store(given_ref, kept_ref))


def finish(row_scale, totals_ref, fact_weight_ref, dim_weight_ref, fact_ref, dim_ref):
    width = fact_ref.shape[0]
    fact_ref[...] = totals_ref[pl.ds(0, width), :] * row_scale + ridge_weight * fact_weight_ref[
        ...
    ].astype(f32)
    dim_ref[...] = totals_ref[
        pl.ds(width, dim_ref.shape[0]), :
    ] * row_scale + ridge_weight * dim_weight_ref[...].astype(f32)


def kernel_call(body, outs, *operands):
    vmem = pl.BlockSpec(memory_space=pltpu.VMEM)
    return pl.pallas_call(
        body,
        out_shape=tuple(jax.ShapeDtypeStruct(shape, dtype) for shape, dtype in outs),
        in_specs=[vmem] * len(operands),
        out_specs=(vmem,) * len(outs),
        compiler_params=pltpu.CompilerParams(vmem_limit_bytes=32 << 20),
    )(*operands)


def on_device(
    fact_features, targets, fact_keys, fill_counts, dim_features, fact_weight, dim_weight
):
    key_devices = lax.axis_size("key")
    fact_devices = lax.axis_size("fact")
    one_z, one_y, near, far, chip, plane = groups_of(fact_devices, key_devices)
    slot_count = fact_keys.shape[0]
    bucket_rows = slot_count // key_devices
    own_keys, dim_width = dim_features.shape
    fact_width, out_width = fact_weight.shape
    ring_keys = len(one_z) * own_keys

    packed = pl.pallas_call(
        functools.partial(pack_slots, own_keys, ring_keys),
        out_shape=jax.ShapeDtypeStruct(
            (key_devices, bucket_rows + extra_rows, fact_width + out_width), bf16
        ),
        in_specs=[pl.BlockSpec(memory_space=pl.ANY)] * 4,
        out_specs=pl.BlockSpec(memory_space=pl.ANY),
        scratch_shapes=[
            pltpu.VMEM((key_devices, bucket_rows), i32),
            pltpu.SMEM((1, key_devices), i32),
            pltpu.VMEM((key_devices, bucket_rows + extra_rows, fact_width + out_width), bf16),
            pltpu.SemaphoreType.DMA((key_devices // 2 + 1, 3)),
        ],
    )(
        fact_keys.reshape(key_devices, bucket_rows),
        fill_counts,
        fact_features.reshape(key_devices, bucket_rows, fact_width),
        targets.reshape(key_devices, bucket_rows, out_width),
    )
    slots = spread(packed, "key")
    rows = lax.all_gather(dim_features, "fact", axis=0, tiled=True, axis_index_groups=near)
    (own,) = kernel_call(own_term, (((fact_width, out_width), f32),), packed, fact_weight)

    block = (ring_size, ring_keys + extra_rows, fact_width + out_width)
    outs = ((block, bf16), (rows.shape, bf16), (own.shape, f32))
    met, rows, own = kernel_call(sum_by_key, outs, slots, rows, own)
    met = spread(met, "fact", one_z)
    rows = lax.all_gather(rows, "fact", axis=0, tiled=True, axis_index_groups=far)
    half = (((fact_width + dim_width) // 2, out_width), f32)
    kept, given = kernel_call(both_terms, (half, half), own, fact_weight, rows, dim_weight, met)
    totals = total_over_devices(kept, given, one_y, chip, plane)
    total_rows = slot_count * fact_devices * key_devices
    row_scale = float(total_rows) ** (-0.5)
    vmem = pl.BlockSpec(memory_space=pltpu.VMEM)
    return tuple(
        pl.pallas_call(
            functools.partial(finish, row_scale),
            out_shape=(
                jax.ShapeDtypeStruct((fact_width, out_width), f32),
                jax.ShapeDtypeStruct((dim_width, out_width), f32),
            ),
            in_specs=[vmem] * 3,
            out_specs=(vmem, vmem),
            compiler_params=pltpu.CompilerParams(vmem_limit_bytes=16 << 20),
        )(totals, fact_weight, dim_weight)
    )


def solution(mesh):
    placed = (
        P(("fact", "key"), None),
        P(("fact", "key"), None),
        P(("fact", "key")),
        P(("fact", "key"), None),
        P(("fact", "key"), None),
        P(),
        P(),
    )
    return jax.shard_map(
        on_device, mesh=mesh, in_specs=placed, out_specs=(P(), P()), check_vma=False
    )
```

```python
import functools

import jax
import jax.numpy as jnp
from jax import lax
from jax.experimental import pallas as pl
from jax.experimental.pallas import tpu as pltpu
from jax.sharding import PartitionSpec as P

ridge_weight = 4.0
ring_size = 8
digit = 64
extra_rows = 8
f32, bf16, i32 = jnp.float32, jnp.bfloat16, jnp.int32


def groups_of(fact_devices, key_devices):
    levels = range(fact_devices // ring_size)
    chips, cores = range(key_devices // 2), range(2)
    one_z = [[z * ring_size + y for y in range(ring_size)] for z in levels]
    one_y = [[z * ring_size + y for z in levels] for y in range(ring_size)]
    chip = [[2 * x + core for core in cores] for x in chips]
    plane = [
        [(z * ring_size + y) * key_devices + 2 * x + core for y in range(ring_size) for x in chips]
        for z in levels
        for core in cores
    ]
    return one_z, one_y, chip, plane


def spread(array, axis, groups=None):
    return lax.all_to_all(
        array, axis, split_axis=0, concat_axis=0, tiled=True, axis_index_groups=groups
    )


def collect(array, axis, copies, groups):
    return spread(jnp.broadcast_to(array[None], (copies, *array.shape)), axis, groups)


def total_over_devices(kept, given, one_y, chip, plane):
    rows, width = kept.shape
    both = ("fact", "key")
    members = len(plane[0])
    swap = [(a, b) for pair in chip for a, b in (pair, pair[::-1])]
    part = kept + lax.ppermute(given, "key", swap)
    part = spread(part.reshape(members, -1, 4, width), both, plane).sum(axis=0)
    part = collect(part, "fact", len(one_y[0]), one_y).sum(axis=0)
    part = collect(part, both, members, plane).reshape(-1, 4, width)
    part = lax.all_gather(part, "key", axis=0, tiled=True, axis_index_groups=chip)
    return part.reshape(2 * rows, width)


def pack_slots(
    own_keys, ring_keys, keys_hbm, fill_hbm, features_hbm, targets_hbm, out_hbm, keys_ref, fill_ref, slots_ref, done
):
    buckets, bucket_rows, width = features_hbm.shape
    out_width = targets_hbm.shape[2]
    slots = pl.ds(0, bucket_rows)
    groups = range(buckets // 2)

    def copies(g):
        two = pl.ds(2 * g, 2)
        return (
            pltpu.make_async_copy(
                features_hbm.at[two], slots_ref.at[two, slots, pl.ds(0, width)], done.at[g, 0]
            ),
            pltpu.make_async_copy(
                targets_hbm.at[two], slots_ref.at[two, slots, pl.ds(width, out_width)], done.at[g, 1]
            ),
            pltpu.make_async_copy(slots_ref.at[two], out_hbm.at[two], done.at[g, 2]),
        )

    keys_in = pltpu.make_async_copy(keys_hbm, keys_ref, done.at[len(groups), 0])
    fill_in = pltpu.make_async_copy(fill_hbm, fill_ref, done.at[len(groups), 1])
    keys_in.start()
    fill_in.start()
    plan = [copies(g) for g in groups]
    for features_in, targets_in, _ in plan:
        features_in.start()
        targets_in.start()
    keys_in.wait()
    fill_in.wait()
    keys = keys_ref[...]
    owner = keys // (own_keys * buckets)
    places = (owner % ring_size) * ring_keys + (owner // ring_size) * own_keys + keys % own_keys
    slot = lax.broadcasted_iota(i32, (1, bucket_rows), 1)
    for b in range(buckets):
        codes = jnp.where(slot < fill_ref[0, b], places[b : b + 1], -digit)
        high = codes // digit
        low = codes - high * digit
        digits = jnp.concatenate([high, low, jnp.zeros_like(high)], axis=1).astype(f32)
        digits = jnp.broadcast_to(digits, (extra_rows, width + out_width))
        slots_ref[b, pl.ds(bucket_rows, extra_rows), :] = digits.astype(bf16)
    for features_in, targets_in, out in plan:
        features_in.wait()
        targets_in.wait()
        out.start()
    for _, _, out in plan:
        out.wait()


def codes_of(packed_ref, b):
    bucket_rows = packed_ref.shape[1] - extra_rows
    digits = packed_ref[b, pl.ds(bucket_rows, extra_rows), :].astype(f32)
    codes = digits[:, :bucket_rows] * digit + digits[:, bucket_rows : 2 * bucket_rows]
    return codes.astype(i32)[:1]


def partial_of(packed_ref, weight_ref, pair):
    slots = pl.ds(0, packed_ref.shape[1] - extra_rows)
    width = weight_ref.shape[0]
    rows = jnp.concatenate([packed_ref[b, slots, :] for b in pair], axis=0)
    features = rows[:, :width]
    value = jnp.dot(features, weight_ref[...], preferred_element_type=f32)
    return features, value - rows[:, width:].astype(f32)


def pairs_of(packed_ref):
    return [(b, b + 1) for b in range(0, packed_ref.shape[0], 2)]


def diagonal_of(rows, columns):
    return lax.broadcasted_iota(i32, (rows, columns), 0) == lax.broadcasted_iota(
        i32, (rows, columns), 1
    )


def sum_by_key(packed_ref, weight_ref, rows_ref, dim_weight_ref, out_ref):
    members, _, two_widths = out_ref.shape
    out_width = two_widths // 2
    ring_keys = rows_ref.shape[0]
    two_rows = 2 * (packed_ref.shape[1] - extra_rows)
    places = lax.broadcasted_iota(i32, (members * ring_keys, two_rows), 0)
    ones = jnp.ones((two_rows, out_width), bf16)
    sums = jnp.zeros((members * ring_keys, two_widths), f32)
    for pair in pairs_of(packed_ref):
        codes = jnp.concatenate([codes_of(packed_ref, b) for b in pair], axis=1)
        one_hot = jnp.where(places == codes, f32(1.0), f32(0.0)).astype(bf16)
        _, value = partial_of(packed_ref, weight_ref, pair)
        value = jnp.concatenate([value.astype(bf16), ones], axis=1)
        sums += jnp.dot(one_hot, value, preferred_element_type=f32)
    values = jnp.dot(rows_ref[...], dim_weight_ref[...], preferred_element_type=f32).astype(bf16)
    diagonal = diagonal_of(ring_keys, out_width)
    own = pl.ds(0, ring_keys)
    for m in range(members):
        part = sums[m * ring_keys : (m + 1) * ring_keys]
        out_ref[m, own, pl.ds(0, out_width)] = part[:, :out_width].astype(bf16)
        out_ref[m, own, pl.ds(out_width, out_width)] = values
        counts = jnp.where(diagonal, part[:, out_width:], f32(0.0)).sum(axis=0, keepdims=True)
        high = jnp.floor(counts * (1.0 / digit))
        digits = jnp.concatenate([high, counts - high * digit], axis=1)
        digits = jnp.broadcast_to(digits, (extra_rows, two_widths))
        out_ref[m, pl.ds(ring_keys, extra_rows), :] = digits.astype(bf16)


def split(value):
    high = value.astype(bf16)
    return high, (value - high.astype(f32)).astype(bf16)


contract = (((0,), (0,)), ((), ()))


def own_term(packed_ref, weight_ref, term_ref, one_hot_ref):
    buckets = packed_ref.shape[0]
    bucket_rows = packed_ref.shape[1] - extra_rows
    out_width = weight_ref.shape[1]
    codes = jnp.concatenate([codes_of(packed_ref, b) for b in range(buckets)], axis=0)
    codes = jnp.transpose(codes.astype(f32)).astype(i32)
    places = lax.broadcasted_iota(i32, (bucket_rows, one_hot_ref.shape[1]), 1)
    total = jnp.zeros((weight_ref.shape[0], 2 * out_width), f32)
    for pair in pairs_of(packed_ref):
        for b in pair:
            one_hot = jnp.where(places == codes[:, b : b + 1], f32(1.0), f32(0.0))
            one_hot_ref[pl.ds(b * bucket_rows, bucket_rows), :] = one_hot.astype(bf16)
        features, value = partial_of(packed_ref, weight_ref, pair)
        live = jnp.concatenate([codes[:, b : b + 1] for b in pair], axis=0) >= 0
        value = jnp.concatenate(split(jnp.where(live, value, f32(0.0))), axis=1)
        total += lax.dot_general(features, value, contract, preferred_element_type=f32)
    term_ref[...] = total[:, :out_width] + total[:, out_width:]


def both_terms(packed_ref, own_ref, one_hot_ref, rows_ref, met_ref, kept_ref, given_ref):
    members, _, two_widths = met_ref.shape
    out_width = two_widths // 2
    ring_keys = rows_ref.shape[0]
    slots = pl.ds(0, packed_ref.shape[1] - extra_rows)
    width = own_ref.shape[0]

    own = pl.ds(0, ring_keys)
    values = jnp.concatenate(
        [met_ref[m, own, pl.ds(out_width, out_width)] for m in range(members)], axis=0
    )
    found = jnp.dot(one_hot_ref[...], values, preferred_element_type=f32).astype(bf16)
    features = jnp.concatenate(
        [packed_ref[b, slots, pl.ds(0, width)] for b in range(packed_ref.shape[0])], axis=0
    )
    fact_term = lax.dot_general(features, found, contract, preferred_element_type=f32)
    fact_term += own_ref[...]

    me = lax.rem(lax.axis_index("fact"), ring_size)
    sums = jnp.zeros((ring_keys, out_width), f32)
    digits = jnp.zeros((extra_rows, two_widths), f32)
    for m in range(members):
        sums += met_ref[m, own, pl.ds(0, out_width)].astype(f32)
        digits += met_ref[m, pl.ds(ring_keys, extra_rows), :].astype(f32)
    counts = digits[:1, :out_width] * digit + digits[:1, out_width:]
    diagonal = diagonal_of(ring_keys, out_width)
    counts = jnp.sum(jnp.where(diagonal, counts, f32(0.0)), axis=1, keepdims=True)
    sums += counts * met_ref[me, own, pl.ds(out_width, out_width)].astype(f32)
    sums = jnp.concatenate(split(sums), axis=1)
    dim_term = lax.dot_general(rows_ref[...], sums, contract, preferred_element_type=f32)
    dim_term = dim_term[:, :out_width] + dim_term[:, out_width:]
    half = kept_ref.shape[0]

    def store(upper_ref, lower_ref):
        upper_ref[pl.ds(0, width), :] = fact_term
        upper_ref[pl.ds(width, half - width), :] = dim_term[: half - width]
        lower_ref[...] = dim_term[half - width :]

    core = lax.rem(lax.axis_index("key"), 2)
    pl.when(core == 0)(lambda: store(kept_ref, given_ref))
    pl.when(core == 1)(lambda: store(given_ref, kept_ref))


def finish(row_scale, totals_ref, fact_weight_ref, dim_weight_ref, fact_ref, dim_ref):
    width = fact_ref.shape[0]
    fact_ref[...] = totals_ref[pl.ds(0, width), :] * row_scale + ridge_weight * fact_weight_ref[
        ...
    ].astype(f32)
    dim_ref[...] = totals_ref[
        pl.ds(width, dim_ref.shape[0]), :
    ] * row_scale + ridge_weight * dim_weight_ref[...].astype(f32)


def kernel_call(body, outs, *operands):
    vmem = pl.BlockSpec(memory_space=pltpu.VMEM)
    return pl.pallas_call(
        body,
        out_shape=tuple(jax.ShapeDtypeStruct(shape, dtype) for shape, dtype in outs),
        in_specs=[vmem] * len(operands),
        out_specs=(vmem,) * len(outs),
        compiler_params=pltpu.CompilerParams(vmem_limit_bytes=32 << 20),
    )(*operands)


def on_device(
    fact_features, targets, fact_keys, fill_counts, dim_features, fact_weight, dim_weight
):
    key_devices = lax.axis_size("key")
    fact_devices = lax.axis_size("fact")
    one_z, one_y, chip, plane = groups_of(fact_devices, key_devices)
    slot_count = fact_keys.shape[0]
    bucket_rows = slot_count // key_devices
    own_keys, dim_width = dim_features.shape
    fact_width, out_width = fact_weight.shape
    ring_keys = len(one_z) * own_keys

    packed = pl.pallas_call(
        functools.partial(pack_slots, own_keys, ring_keys),
        out_shape=jax.ShapeDtypeStruct(
            (key_devices, bucket_rows + extra_rows, fact_width + out_width), bf16
        ),
        in_specs=[pl.BlockSpec(memory_space=pl.ANY)] * 4,
        out_specs=pl.BlockSpec(memory_space=pl.ANY),
        scratch_shapes=[
            pltpu.VMEM((key_devices, bucket_rows), i32),
            pltpu.SMEM((1, key_devices), i32),
            pltpu.VMEM((key_devices, bucket_rows + extra_rows, fact_width + out_width), bf16),
            pltpu.SemaphoreType.DMA((key_devices // 2 + 1, 3)),
        ],
    )(
        fact_keys.reshape(key_devices, bucket_rows),
        fill_counts,
        fact_features.reshape(key_devices, bucket_rows, fact_width),
        targets.reshape(key_devices, bucket_rows, out_width),
    )
    packed = spread(packed, "key")
    rows = lax.all_gather(dim_features, "fact", axis=0, tiled=True, axis_index_groups=one_y)

    block = (ring_size, ring_keys + extra_rows, 2 * out_width)
    (met,) = kernel_call(sum_by_key, ((block, bf16),), packed, fact_weight, rows, dim_weight)
    met = spread(met, "fact", one_z)
    outs = (((fact_width, out_width), f32), ((slot_count, ring_size * ring_keys), bf16))
    own, one_hot = kernel_call(own_term, outs, packed, fact_weight)
    half = (((fact_width + dim_width) // 2, out_width), f32)
    kept, given = kernel_call(both_terms, (half, half), packed, own, one_hot, rows, met)
    totals = total_over_devices(kept, given, one_y, chip, plane)
    total_rows = slot_count * fact_devices * key_devices
    row_scale = float(total_rows) ** (-0.5)
    vmem = pl.BlockSpec(memory_space=pltpu.VMEM)
    return tuple(
        pl.pallas_call(
            functools.partial(finish, row_scale),
            out_shape=(
                jax.ShapeDtypeStruct((fact_width, out_width), f32),
                jax.ShapeDtypeStruct((dim_width, out_width), f32),
            ),
            in_specs=[vmem] * 3,
            out_specs=(vmem, vmem),
            compiler_params=pltpu.CompilerParams(vmem_limit_bytes=16 << 20),
        )(totals, fact_weight, dim_weight)
    )


def solution(mesh):
    placed = (
        P(("fact", "key"), None),
        P(("fact", "key"), None),
        P(("fact", "key")),
        P(("fact", "key"), None),
        P(("fact", "key"), None),
        P(),
        P(),
    )
    return jax.shard_map(
        on_device, mesh=mesh, in_specs=placed, out_specs=(P(), P()), check_vma=False
    )
```

```python
import functools

import jax
import jax.numpy as jnp
from jax import lax
from jax.experimental import pallas as pl
from jax.experimental.pallas import tpu as pltpu
from jax.sharding import PartitionSpec as P

ridge_weight = 4.0
ring_size = 8
digit = 64
extra_rows = 8
f32, bf16, i32 = jnp.float32, jnp.bfloat16, jnp.int32


def groups_of(fact_devices, key_devices):
    levels = range(fact_devices // ring_size)
    chips, cores = range(key_devices // 2), range(2)
    one_z = [[z * ring_size + y for y in range(ring_size)] for z in levels]
    one_y = [[z * ring_size + y for z in levels] for y in range(ring_size)]
    chip = [[2 * x + core for core in cores] for x in chips]
    plane = [
        [(z * ring_size + y) * key_devices + 2 * x + core for x in chips for y in range(ring_size)]
        for z in levels
        for core in cores
    ]
    return one_z, one_y, chip, plane


def spread(array, axis, groups=None):
    return lax.all_to_all(
        array, axis, split_axis=0, concat_axis=0, tiled=True, axis_index_groups=groups
    )


def collect(array, axis, copies, groups):
    return spread(jnp.broadcast_to(array[None], (copies, *array.shape)), axis, groups)


def total_over_devices(kept, given, one_y, chip, plane):
    rows, width = kept.shape
    both = ("fact", "key")
    members = len(plane[0])
    swap = [(a, b) for pair in chip for a, b in (pair, pair[::-1])]
    part = kept + lax.ppermute(given, "key", swap)
    part = spread(part.reshape(members, -1, 4, width), both, plane).sum(axis=0)
    part = collect(part, "fact", len(one_y[0]), one_y).sum(axis=0)
    part = collect(part, both, members, plane).reshape(-1, 4, width)
    part = lax.all_gather(part, "key", axis=0, tiled=True, axis_index_groups=chip)
    return part.reshape(2 * rows, width)


def pack_slots(
    own_keys, ring_keys, keys_hbm, fill_hbm, features_hbm, targets_hbm, out_hbm, keys_ref, fill_ref, slots_ref, done
):
    buckets, bucket_rows, width = features_hbm.shape
    out_width = targets_hbm.shape[2]
    slots = pl.ds(0, bucket_rows)
    groups = range(buckets // 2)

    def copies(g):
        two = pl.ds(2 * g, 2)
        return (
            pltpu.make_async_copy(
                features_hbm.at[two], slots_ref.at[two, slots, pl.ds(0, width)], done.at[g, 0]
            ),
            pltpu.make_async_copy(
                targets_hbm.at[two], slots_ref.at[two, slots, pl.ds(width, out_width)], done.at[g, 1]
            ),
            pltpu.make_async_copy(slots_ref.at[two], out_hbm.at[two], done.at[g, 2]),
        )

    keys_in = pltpu.make_async_copy(keys_hbm, keys_ref, done.at[len(groups), 0])
    fill_in = pltpu.make_async_copy(fill_hbm, fill_ref, done.at[len(groups), 1])
    keys_in.start()
    fill_in.start()
    plan = [copies(g) for g in groups]
    for features_in, targets_in, _ in plan:
        features_in.start()
        targets_in.start()
    keys_in.wait()
    fill_in.wait()
    keys = keys_ref[...]
    owner = keys // (own_keys * buckets)
    places = (owner % ring_size) * ring_keys + (owner // ring_size) * own_keys + keys % own_keys
    slot = lax.broadcasted_iota(i32, (1, bucket_rows), 1)
    for b in range(buckets):
        codes = jnp.where(slot < fill_ref[0, b], places[b : b + 1], -digit)
        high = codes // digit
        low = codes - high * digit
        digits = jnp.concatenate([high, low, jnp.zeros_like(high)], axis=1).astype(f32)
        digits = jnp.broadcast_to(digits, (extra_rows, width + out_width))
        slots_ref[b, pl.ds(bucket_rows, extra_rows), :] = digits.astype(bf16)
    for features_in, targets_in, out in plan:
        features_in.wait()
        targets_in.wait()
        out.start()
    for _, _, out in plan:
        out.wait()


def codes_of(packed_ref, b):
    bucket_rows = packed_ref.shape[1] - extra_rows
    digits = packed_ref[b, pl.ds(bucket_rows, extra_rows), :].astype(f32)
    codes = digits[:, :bucket_rows] * digit + digits[:, bucket_rows : 2 * bucket_rows]
    return codes.astype(i32)[:1]


def partial_of(packed_ref, weight_ref, pair):
    slots = pl.ds(0, packed_ref.shape[1] - extra_rows)
    width = weight_ref.shape[0]
    rows = jnp.concatenate([packed_ref[b, slots, :] for b in pair], axis=0)
    features = rows[:, :width]
    value = jnp.dot(features, weight_ref[...], preferred_element_type=f32)
    return features, value - rows[:, width:].astype(f32)


def pairs_of(packed_ref):
    return [(b, b + 1) for b in range(0, packed_ref.shape[0], 2)]


def diagonal_of(rows, columns):
    return lax.broadcasted_iota(i32, (rows, columns), 0) == lax.broadcasted_iota(
        i32, (rows, columns), 1
    )


def sum_by_key(packed_ref, weight_ref, rows_ref, dim_weight_ref, out_ref):
    members, _, two_widths = out_ref.shape
    out_width = two_widths // 2
    ring_keys = rows_ref.shape[0]
    two_rows = 2 * (packed_ref.shape[1] - extra_rows)
    places = lax.broadcasted_iota(i32, (members * ring_keys, two_rows), 0)
    ones = jnp.ones((two_rows, out_width), bf16)
    sums = jnp.zeros((members * ring_keys, two_widths), f32)
    for pair in pairs_of(packed_ref):
        codes = jnp.concatenate([codes_of(packed_ref, b) for b in pair], axis=1)
        one_hot = jnp.where(places == codes, f32(1.0), f32(0.0)).astype(bf16)
        _, value = partial_of(packed_ref, weight_ref, pair)
        value = jnp.concatenate([value.astype(bf16), ones], axis=1)
        sums += jnp.dot(one_hot, value, preferred_element_type=f32)
    values = jnp.dot(rows_ref[...], dim_weight_ref[...], preferred_element_type=f32).astype(bf16)
    diagonal = diagonal_of(ring_keys, out_width)
    own = pl.ds(0, ring_keys)
    for m in range(members):
        part = sums[m * ring_keys : (m + 1) * ring_keys]
        out_ref[m, own, pl.ds(0, out_width)] = part[:, :out_width].astype(bf16)
        out_ref[m, own, pl.ds(out_width, out_width)] = values
        counts = jnp.where(diagonal, part[:, out_width:], f32(0.0)).sum(axis=0, keepdims=True)
        high = jnp.floor(counts * (1.0 / digit))
        digits = jnp.concatenate([high, counts - high * digit], axis=1)
        digits = jnp.broadcast_to(digits, (extra_rows, two_widths))
        out_ref[m, pl.ds(ring_keys, extra_rows), :] = digits.astype(bf16)


def both_terms(packed_ref, weight_ref, rows_ref, met_ref, kept_ref, given_ref):
    members, _, two_widths = met_ref.shape
    out_width = two_widths // 2
    ring_keys = rows_ref.shape[0]
    buckets = packed_ref.shape[0]
    bucket_rows = packed_ref.shape[1] - extra_rows
    width = weight_ref.shape[0]
    contract = (((0,), (0,)), ((), ()))

    own = pl.ds(0, ring_keys)
    values = jnp.concatenate(
        [met_ref[m, own, pl.ds(out_width, out_width)] for m in range(members)], axis=0
    )
    codes = jnp.concatenate([codes_of(packed_ref, b) for b in range(buckets)], axis=0)
    codes = jnp.transpose(codes.astype(f32)).astype(i32)
    places = lax.broadcasted_iota(i32, (bucket_rows, members * ring_keys), 1)
    fact_term = jnp.zeros((width, out_width), f32)
    for pair in pairs_of(packed_ref):
        one_hot = [
            jnp.where(places == codes[:, b : b + 1], f32(1.0), f32(0.0)).astype(bf16) for b in pair
        ]
        features, value = partial_of(packed_ref, weight_ref, pair)
        found = jnp.dot(jnp.concatenate(one_hot, axis=0), values, preferred_element_type=f32)
        live = jnp.concatenate([codes[:, b : b + 1] for b in pair], axis=0) >= 0
        residual = jnp.where(live, value + found, f32(0.0)).astype(bf16)
        fact_term += lax.dot_general(features, residual, contract, preferred_element_type=f32)
    me = lax.rem(lax.axis_index("fact"), ring_size)
    sums = jnp.zeros((ring_keys, out_width), f32)
    digits = jnp.zeros((extra_rows, two_widths), f32)
    for m in range(members):
        sums += met_ref[m, own, pl.ds(0, out_width)].astype(f32)
        digits += met_ref[m, pl.ds(ring_keys, extra_rows), :].astype(f32)
    counts = digits[:1, :out_width] * digit + digits[:1, out_width:]
    diagonal = diagonal_of(ring_keys, out_width)
    counts = jnp.sum(jnp.where(diagonal, counts, f32(0.0)), axis=1, keepdims=True)
    sums += counts * met_ref[me, own, pl.ds(out_width, out_width)].astype(f32)
    high = sums.astype(bf16)
    low = (sums - high.astype(f32)).astype(bf16)
    dim_term = lax.dot_general(
        rows_ref[...], jnp.concatenate([high, low], axis=1), contract, preferred_element_type=f32
    )
    dim_term = dim_term[:, :out_width] + dim_term[:, out_width:]
    half = kept_ref.shape[0]

    def store(upper_ref, lower_ref):
        upper_ref[pl.ds(0, width), :] = fact_term
        upper_ref[pl.ds(width, half - width), :] = dim_term[: half - width]
        lower_ref[...] = dim_term[half - width :]

    core = lax.rem(lax.axis_index("key"), 2)
    pl.when(core == 0)(lambda: store(kept_ref, given_ref))
    pl.when(core == 1)(lambda: store(given_ref, kept_ref))


def finish(row_scale, totals_ref, fact_weight_ref, dim_weight_ref, fact_ref, dim_ref):
    width = fact_ref.shape[0]
    fact_ref[...] = totals_ref[pl.ds(0, width), :] * row_scale + ridge_weight * fact_weight_ref[
        ...
    ].astype(f32)
    dim_ref[...] = totals_ref[
        pl.ds(width, dim_ref.shape[0]), :
    ] * row_scale + ridge_weight * dim_weight_ref[...].astype(f32)


def kernel_call(body, shapes, dtype, *operands):
    vmem = pl.BlockSpec(memory_space=pltpu.VMEM)
    return pl.pallas_call(
        body,
        out_shape=tuple(jax.ShapeDtypeStruct(shape, dtype) for shape in shapes),
        in_specs=[vmem] * len(operands),
        out_specs=(vmem,) * len(shapes),
        compiler_params=pltpu.CompilerParams(vmem_limit_bytes=32 << 20),
    )(*operands)


def on_device(
    fact_features, targets, fact_keys, fill_counts, dim_features, fact_weight, dim_weight
):
    key_devices = lax.axis_size("key")
    fact_devices = lax.axis_size("fact")
    one_z, one_y, chip, plane = groups_of(fact_devices, key_devices)
    slot_count = fact_keys.shape[0]
    bucket_rows = slot_count // key_devices
    own_keys, dim_width = dim_features.shape
    fact_width, out_width = fact_weight.shape
    ring_keys = len(one_z) * own_keys

    packed = pl.pallas_call(
        functools.partial(pack_slots, own_keys, ring_keys),
        out_shape=jax.ShapeDtypeStruct(
            (key_devices, bucket_rows + extra_rows, fact_width + out_width), bf16
        ),
        in_specs=[pl.BlockSpec(memory_space=pl.ANY)] * 4,
        out_specs=pl.BlockSpec(memory_space=pl.ANY),
        scratch_shapes=[
            pltpu.VMEM((key_devices, bucket_rows), i32),
            pltpu.SMEM((1, key_devices), i32),
            pltpu.VMEM((key_devices, bucket_rows + extra_rows, fact_width + out_width), bf16),
            pltpu.SemaphoreType.DMA((key_devices // 2 + 1, 3)),
        ],
    )(
        fact_keys.reshape(key_devices, bucket_rows),
        fill_counts,
        fact_features.reshape(key_devices, bucket_rows, fact_width),
        targets.reshape(key_devices, bucket_rows, out_width),
    )
    packed = spread(packed, "key")
    rows = lax.all_gather(dim_features, "fact", axis=0, tiled=True, axis_index_groups=one_y)

    (met,) = kernel_call(
        sum_by_key,
        ((ring_size, ring_keys + extra_rows, 2 * out_width),),
        bf16,
        packed,
        fact_weight,
        rows,
        dim_weight,
    )
    met = spread(met, "fact", one_z)
    half = ((fact_width + dim_width) // 2, out_width)
    kept, given = kernel_call(both_terms, (half, half), f32, packed, fact_weight, rows, met)
    totals = total_over_devices(kept, given, one_y, chip, plane)
    total_rows = slot_count * fact_devices * key_devices
    row_scale = float(total_rows) ** (-0.5)
    vmem = pl.BlockSpec(memory_space=pltpu.VMEM)
    return tuple(
        pl.pallas_call(
            functools.partial(finish, row_scale),
            out_shape=(
                jax.ShapeDtypeStruct((fact_width, out_width), f32),
                jax.ShapeDtypeStruct((dim_width, out_width), f32),
            ),
            in_specs=[vmem] * 3,
            out_specs=(vmem, vmem),
            compiler_params=pltpu.CompilerParams(vmem_limit_bytes=16 << 20),
        )(totals, fact_weight, dim_weight)
    )


def solution(mesh):
    placed = (
        P(("fact", "key"), None),
        P(("fact", "key"), None),
        P(("fact", "key")),
        P(("fact", "key"), None),
        P(("fact", "key"), None),
        P(),
        P(),
    )
    return jax.shard_map(
        on_device, mesh=mesh, in_specs=placed, out_specs=(P(), P()), check_vma=False
    )
```

```python
import functools

import jax
import jax.numpy as jnp
from jax import lax
from jax.experimental import pallas as pl
from jax.experimental.pallas import tpu as pltpu
from jax.sharding import PartitionSpec as P

ridge_weight = 4.0
ring_size = 8
digit = 64
extra_rows = 8
f32, bf16, i32 = jnp.float32, jnp.bfloat16, jnp.int32


def groups_of(fact_devices, key_devices):
    levels = range(fact_devices // ring_size)
    chips, cores = range(key_devices // 2), range(2)
    one_z = [[z * ring_size + y for y in range(ring_size)] for z in levels]
    one_y = [[z * ring_size + y for z in levels] for y in range(ring_size)]
    chip = [[2 * x + core for core in cores] for x in chips]
    plane = [
        [(z * ring_size + y) * key_devices + 2 * x + core for x in chips for y in range(ring_size)]
        for z in levels
        for core in cores
    ]
    return one_z, one_y, chip, plane


def spread(array, axis, groups=None):
    return lax.all_to_all(
        array, axis, split_axis=0, concat_axis=0, tiled=True, axis_index_groups=groups
    )


def collect(array, axis, copies, groups):
    return spread(jnp.broadcast_to(array[None], (copies, *array.shape)), axis, groups)


def total_over_devices(kept, given, one_y, chip, plane):
    rows, width = kept.shape
    both = ("fact", "key")
    members = len(plane[0])
    swap = [(a, b) for pair in chip for a, b in (pair, pair[::-1])]
    part = kept + lax.ppermute(given, "key", swap)
    part = spread(part.reshape(members, -1, 4, width), both, plane).sum(axis=0)
    part = collect(part, "fact", len(one_y[0]), one_y).sum(axis=0)
    rings = members // ring_size
    back = [[line[x * ring_size + y] for y in range(ring_size) for x in range(rings)] for line in plane]
    part = collect(part, both, members, back).reshape(ring_size, rings, *part.shape)
    part = part.swapaxes(0, 1).reshape(-1, 4, width)
    part = lax.all_gather(part, "key", axis=0, tiled=True, axis_index_groups=chip)
    return part.reshape(2 * rows, width)


def pack_slots(
    own_keys, ring_keys, keys_hbm, fill_hbm, features_hbm, targets_hbm, out_hbm, keys_ref, fill_ref, slots_ref, done
):
    buckets, bucket_rows, width = features_hbm.shape
    out_width = targets_hbm.shape[2]
    slots = pl.ds(0, bucket_rows)
    groups = range(buckets // 2)

    def copies(g):
        two = pl.ds(2 * g, 2)
        return (
            pltpu.make_async_copy(
                features_hbm.at[two], slots_ref.at[two, slots, pl.ds(0, width)], done.at[g, 0]
            ),
            pltpu.make_async_copy(
                targets_hbm.at[two], slots_ref.at[two, slots, pl.ds(width, out_width)], done.at[g, 1]
            ),
            pltpu.make_async_copy(slots_ref.at[two], out_hbm.at[two], done.at[g, 2]),
        )

    keys_in = pltpu.make_async_copy(keys_hbm, keys_ref, done.at[len(groups), 0])
    fill_in = pltpu.make_async_copy(fill_hbm, fill_ref, done.at[len(groups), 1])
    keys_in.start()
    fill_in.start()
    plan = [copies(g) for g in groups]
    for features_in, targets_in, _ in plan:
        features_in.start()
        targets_in.start()
    keys_in.wait()
    fill_in.wait()
    keys = keys_ref[...]
    owner = keys // (own_keys * buckets)
    places = (owner % ring_size) * ring_keys + (owner // ring_size) * own_keys + keys % own_keys
    slot = lax.broadcasted_iota(i32, (1, bucket_rows), 1)
    for b in range(buckets):
        codes = jnp.where(slot < fill_ref[0, b], places[b : b + 1], -digit)
        high = codes // digit
        low = codes - high * digit
        digits = jnp.concatenate([high, low, jnp.zeros_like(high)], axis=1).astype(f32)
        digits = jnp.broadcast_to(digits, (extra_rows, width + out_width))
        slots_ref[b, pl.ds(bucket_rows, extra_rows), :] = digits.astype(bf16)
    for features_in, targets_in, out in plan:
        features_in.wait()
        targets_in.wait()
        out.start()
    for _, _, out in plan:
        out.wait()


def codes_of(packed_ref, b):
    bucket_rows = packed_ref.shape[1] - extra_rows
    digits = packed_ref[b, pl.ds(bucket_rows, extra_rows), :].astype(f32)
    codes = digits[:, :bucket_rows] * digit + digits[:, bucket_rows : 2 * bucket_rows]
    return codes.astype(i32)[:1]


def partial_of(packed_ref, weight_ref, pair):
    slots = pl.ds(0, packed_ref.shape[1] - extra_rows)
    width = weight_ref.shape[0]
    rows = jnp.concatenate([packed_ref[b, slots, :] for b in pair], axis=0)
    features = rows[:, :width]
    value = jnp.dot(features, weight_ref[...], preferred_element_type=f32)
    return features, value - rows[:, width:].astype(f32)


def pairs_of(packed_ref):
    return [(b, b + 1) for b in range(0, packed_ref.shape[0], 2)]


def diagonal_of(rows, columns):
    return lax.broadcasted_iota(i32, (rows, columns), 0) == lax.broadcasted_iota(
        i32, (rows, columns), 1
    )


def sum_by_key(packed_ref, weight_ref, rows_ref, dim_weight_ref, out_ref):
    members, _, two_widths = out_ref.shape
    out_width = two_widths // 2
    ring_keys = rows_ref.shape[0]
    two_rows = 2 * (packed_ref.shape[1] - extra_rows)
    places = lax.broadcasted_iota(i32, (members * ring_keys, two_rows), 0)
    ones = jnp.ones((two_rows, out_width), bf16)
    sums = jnp.zeros((members * ring_keys, two_widths), f32)
    for pair in pairs_of(packed_ref):
        codes = jnp.concatenate([codes_of(packed_ref, b) for b in pair], axis=1)
        one_hot = jnp.where(places == codes, f32(1.0), f32(0.0)).astype(bf16)
        _, value = partial_of(packed_ref, weight_ref, pair)
        value = jnp.concatenate([value.astype(bf16), ones], axis=1)
        sums += jnp.dot(one_hot, value, preferred_element_type=f32)
    values = jnp.dot(rows_ref[...], dim_weight_ref[...], preferred_element_type=f32).astype(bf16)
    diagonal = diagonal_of(ring_keys, out_width)
    own = pl.ds(0, ring_keys)
    for m in range(members):
        part = sums[m * ring_keys : (m + 1) * ring_keys]
        out_ref[m, own, pl.ds(0, out_width)] = part[:, :out_width].astype(bf16)
        out_ref[m, own, pl.ds(out_width, out_width)] = values
        counts = jnp.where(diagonal, part[:, out_width:], f32(0.0)).sum(axis=0, keepdims=True)
        high = jnp.floor(counts * (1.0 / digit))
        digits = jnp.concatenate([high, counts - high * digit], axis=1)
        digits = jnp.broadcast_to(digits, (extra_rows, two_widths))
        out_ref[m, pl.ds(ring_keys, extra_rows), :] = digits.astype(bf16)


def both_terms(packed_ref, weight_ref, rows_ref, met_ref, kept_ref, given_ref):
    members, _, two_widths = met_ref.shape
    out_width = two_widths // 2
    ring_keys = rows_ref.shape[0]
    buckets = packed_ref.shape[0]
    bucket_rows = packed_ref.shape[1] - extra_rows
    width = weight_ref.shape[0]
    contract = (((0,), (0,)), ((), ()))

    own = pl.ds(0, ring_keys)
    values = jnp.concatenate(
        [met_ref[m, own, pl.ds(out_width, out_width)] for m in range(members)], axis=0
    )
    codes = jnp.concatenate([codes_of(packed_ref, b) for b in range(buckets)], axis=0)
    codes = jnp.transpose(codes.astype(f32)).astype(i32)
    places = lax.broadcasted_iota(i32, (bucket_rows, members * ring_keys), 1)
    fact_term = jnp.zeros((width, out_width), f32)
    for pair in pairs_of(packed_ref):
        one_hot = [
            jnp.where(places == codes[:, b : b + 1], f32(1.0), f32(0.0)).astype(bf16) for b in pair
        ]
        features, value = partial_of(packed_ref, weight_ref, pair)
        found = jnp.dot(jnp.concatenate(one_hot, axis=0), values, preferred_element_type=f32)
        live = jnp.concatenate([codes[:, b : b + 1] for b in pair], axis=0) >= 0
        residual = jnp.where(live, value + found, f32(0.0)).astype(bf16)
        fact_term += lax.dot_general(features, residual, contract, preferred_element_type=f32)
    me = lax.rem(lax.axis_index("fact"), ring_size)
    sums = jnp.zeros((ring_keys, out_width), f32)
    digits = jnp.zeros((extra_rows, two_widths), f32)
    for m in range(members):
        sums += met_ref[m, own, pl.ds(0, out_width)].astype(f32)
        digits += met_ref[m, pl.ds(ring_keys, extra_rows), :].astype(f32)
    counts = digits[:1, :out_width] * digit + digits[:1, out_width:]
    diagonal = diagonal_of(ring_keys, out_width)
    counts = jnp.sum(jnp.where(diagonal, counts, f32(0.0)), axis=1, keepdims=True)
    sums += counts * met_ref[me, own, pl.ds(out_width, out_width)].astype(f32)
    high = sums.astype(bf16)
    low = (sums - high.astype(f32)).astype(bf16)
    dim_term = lax.dot_general(
        rows_ref[...], jnp.concatenate([high, low], axis=1), contract, preferred_element_type=f32
    )
    dim_term = dim_term[:, :out_width] + dim_term[:, out_width:]
    half = kept_ref.shape[0]

    def store(upper_ref, lower_ref):
        upper_ref[pl.ds(0, width), :] = fact_term
        upper_ref[pl.ds(width, half - width), :] = dim_term[: half - width]
        lower_ref[...] = dim_term[half - width :]

    core = lax.rem(lax.axis_index("key"), 2)
    pl.when(core == 0)(lambda: store(kept_ref, given_ref))
    pl.when(core == 1)(lambda: store(given_ref, kept_ref))


def finish(row_scale, totals_ref, fact_weight_ref, dim_weight_ref, fact_ref, dim_ref):
    width = fact_ref.shape[0]
    fact_ref[...] = totals_ref[pl.ds(0, width), :] * row_scale + ridge_weight * fact_weight_ref[
        ...
    ].astype(f32)
    dim_ref[...] = totals_ref[
        pl.ds(width, dim_ref.shape[0]), :
    ] * row_scale + ridge_weight * dim_weight_ref[...].astype(f32)


def kernel_call(body, shapes, dtype, *operands):
    vmem = pl.BlockSpec(memory_space=pltpu.VMEM)
    return pl.pallas_call(
        body,
        out_shape=tuple(jax.ShapeDtypeStruct(shape, dtype) for shape in shapes),
        in_specs=[vmem] * len(operands),
        out_specs=(vmem,) * len(shapes),
        compiler_params=pltpu.CompilerParams(vmem_limit_bytes=32 << 20),
    )(*operands)


def on_device(
    fact_features, targets, fact_keys, fill_counts, dim_features, fact_weight, dim_weight
):
    key_devices = lax.axis_size("key")
    fact_devices = lax.axis_size("fact")
    one_z, one_y, chip, plane = groups_of(fact_devices, key_devices)
    slot_count = fact_keys.shape[0]
    bucket_rows = slot_count // key_devices
    own_keys, dim_width = dim_features.shape
    fact_width, out_width = fact_weight.shape
    ring_keys = len(one_z) * own_keys

    packed = pl.pallas_call(
        functools.partial(pack_slots, own_keys, ring_keys),
        out_shape=jax.ShapeDtypeStruct(
            (key_devices, bucket_rows + extra_rows, fact_width + out_width), bf16
        ),
        in_specs=[pl.BlockSpec(memory_space=pl.ANY)] * 4,
        out_specs=pl.BlockSpec(memory_space=pl.ANY),
        scratch_shapes=[
            pltpu.VMEM((key_devices, bucket_rows), i32),
            pltpu.SMEM((1, key_devices), i32),
            pltpu.VMEM((key_devices, bucket_rows + extra_rows, fact_width + out_width), bf16),
            pltpu.SemaphoreType.DMA((key_devices // 2 + 1, 3)),
        ],
    )(
        fact_keys.reshape(key_devices, bucket_rows),
        fill_counts,
        fact_features.reshape(key_devices, bucket_rows, fact_width),
        targets.reshape(key_devices, bucket_rows, out_width),
    )
    packed = spread(packed, "key")
    rows = lax.all_gather(dim_features, "fact", axis=0, tiled=True, axis_index_groups=one_y)

    (met,) = kernel_call(
        sum_by_key,
        ((ring_size, ring_keys + extra_rows, 2 * out_width),),
        bf16,
        packed,
        fact_weight,
        rows,
        dim_weight,
    )
    met = spread(met, "fact", one_z)
    half = ((fact_width + dim_width) // 2, out_width)
    kept, given = kernel_call(both_terms, (half, half), f32, packed, fact_weight, rows, met)
    totals = total_over_devices(kept, given, one_y, chip, plane)
    total_rows = slot_count * fact_devices * key_devices
    row_scale = float(total_rows) ** (-0.5)
    vmem = pl.BlockSpec(memory_space=pltpu.VMEM)
    return tuple(
        pl.pallas_call(
            functools.partial(finish, row_scale),
            out_shape=(
                jax.ShapeDtypeStruct((fact_width, out_width), f32),
                jax.ShapeDtypeStruct((dim_width, out_width), f32),
            ),
            in_specs=[vmem] * 3,
            out_specs=(vmem, vmem),
            compiler_params=pltpu.CompilerParams(vmem_limit_bytes=16 << 20),
        )(totals, fact_weight, dim_weight)
    )


def solution(mesh):
    placed = (
        P(("fact", "key"), None),
        P(("fact", "key"), None),
        P(("fact", "key")),
        P(("fact", "key"), None),
        P(("fact", "key"), None),
        P(),
        P(),
    )
    return jax.shard_map(
        on_device, mesh=mesh, in_specs=placed, out_specs=(P(), P()), check_vma=False
    )
```

```python
import functools

import jax
import jax.numpy as jnp
from jax import lax
from jax.experimental import pallas as pl
from jax.experimental.pallas import tpu as pltpu
from jax.sharding import PartitionSpec as P

ridge_weight = 4.0
ring_size = 8
digit = 64
extra_rows = 8
f32, bf16, i32, i16 = jnp.float32, jnp.bfloat16, jnp.int32, jnp.int16


def groups_of(fact_devices, key_devices):
    levels = range(fact_devices // ring_size)
    chips, cores = range(key_devices // 2), range(2)
    one_z = [[z * ring_size + y for y in range(ring_size)] for z in levels]
    one_y = [[z * ring_size + y for z in levels] for y in range(ring_size)]
    chip = [[2 * x + core for core in cores] for x in chips]
    plane = [
        [(z * ring_size + y) * key_devices + 2 * x + core for y in range(ring_size) for x in chips]
        for z in levels
        for core in cores
    ]
    return one_z, one_y, chip, plane


def spread(array, axis, groups=None):
    return lax.all_to_all(
        array, axis, split_axis=0, concat_axis=0, tiled=True, axis_index_groups=groups
    )


def collect(array, axis, copies, groups):
    return spread(jnp.broadcast_to(array[None], (copies, *array.shape)), axis, groups)


def total_over_devices(kept, given, one_y, chip, plane):
    rows, width = kept.shape
    both = ("fact", "key")
    members = len(plane[0])
    swap = [(a, b) for pair in chip for a, b in (pair, pair[::-1])]
    part = kept + lax.ppermute(given, "key", swap)
    part = spread(part.reshape(members, -1, 4, width), both, plane).sum(axis=0)
    part = collect(part, "fact", len(one_y[0]), one_y).sum(axis=0)
    part = collect(part, both, members, plane).reshape(-1, 4, width)
    part = lax.all_gather(part, "key", axis=0, tiled=True, axis_index_groups=chip)
    return part.reshape(2 * rows, width)


def pack_slots(
    own_keys, ring_keys, keys_hbm, fill_hbm, features_hbm, targets_hbm, out_hbm, keys_ref, fill_ref, slots_ref, done
):
    buckets, bucket_rows, width = features_hbm.shape
    out_width = targets_hbm.shape[2]
    slots = pl.ds(0, bucket_rows)
    groups = range(buckets // 2)

    def copies(g):
        two = pl.ds(2 * g, 2)
        return (
            pltpu.make_async_copy(
                features_hbm.at[two], slots_ref.at[two, slots, pl.ds(0, width)], done.at[g, 0]
            ),
            pltpu.make_async_copy(
                targets_hbm.at[two], slots_ref.at[two, slots, pl.ds(width, out_width)], done.at[g, 1]
            ),
            pltpu.make_async_copy(slots_ref.at[two], out_hbm.at[two], done.at[g, 2]),
        )

    keys_in = pltpu.make_async_copy(keys_hbm, keys_ref, done.at[len(groups), 0])
    fill_in = pltpu.make_async_copy(fill_hbm, fill_ref, done.at[len(groups), 1])
    keys_in.start()
    fill_in.start()
    plan = [copies(g) for g in groups]
    for features_in, targets_in, _ in plan:
        features_in.start()
        targets_in.start()
    keys_in.wait()
    fill_in.wait()
    keys = keys_ref[...]
    owner = keys // (own_keys * buckets)
    places = (owner % ring_size) * ring_keys + (owner // ring_size) * own_keys + keys % own_keys
    slot = lax.broadcasted_iota(i32, (1, bucket_rows), 1)
    for b in range(buckets):
        codes = jnp.where(slot < fill_ref[0, b], places[b : b + 1], -digit)
        high = codes // digit
        low = codes - high * digit
        digits = jnp.concatenate([high, low, jnp.zeros_like(high)], axis=1).astype(f32)
        digits = jnp.broadcast_to(digits, (extra_rows, width + out_width))
        slots_ref[b, pl.ds(bucket_rows, extra_rows), :] = digits.astype(bf16)
    for features_in, targets_in, out in plan:
        features_in.wait()
        targets_in.wait()
        out.start()
    for _, _, out in plan:
        out.wait()


def codes_of(packed_ref, b):
    bucket_rows = packed_ref.shape[1] - extra_rows
    digits = packed_ref[b, pl.ds(bucket_rows, extra_rows), :].astype(f32)
    codes = digits[:, :bucket_rows] * digit + digits[:, bucket_rows : 2 * bucket_rows]
    return codes.astype(i32)[:1]


def partial_of(packed_ref, weight_ref, pair):
    slots = pl.ds(0, packed_ref.shape[1] - extra_rows)
    width = weight_ref.shape[0]
    rows = jnp.concatenate([packed_ref[b, slots, :] for b in pair], axis=0)
    features = rows[:, :width]
    value = jnp.dot(features, weight_ref[...], preferred_element_type=f32)
    return features, value - rows[:, width:].astype(f32)


def pairs_of(packed_ref):
    return [(b, b + 1) for b in range(0, packed_ref.shape[0], 2)]


def diagonal_of(rows, columns):
    return lax.broadcasted_iota(i32, (rows, columns), 0) == lax.broadcasted_iota(
        i32, (rows, columns), 1
    )


def sum_by_key(packed_ref, weight_ref, rows_ref, dim_weight_ref, out_ref):
    members, _, two_widths = out_ref.shape
    out_width = two_widths // 2
    ring_keys = rows_ref.shape[0]
    two_rows = 2 * (packed_ref.shape[1] - extra_rows)
    places = lax.broadcasted_iota(i32, (members * ring_keys, two_rows), 0).astype(i16)
    places = places.reshape(-1, 16, two_rows)
    ones = jnp.ones((two_rows, out_width), bf16)
    sums = jnp.zeros((members * ring_keys, two_widths), f32)
    for pair in pairs_of(packed_ref):
        codes = jnp.concatenate([codes_of(packed_ref, b) for b in pair], axis=1)
        codes = jnp.broadcast_to(codes, (16, two_rows)).astype(i16)
        one_hot = jnp.where(places == codes[None], bf16(1.0), bf16(0.0))
        one_hot = one_hot.reshape(members * ring_keys, two_rows)
        _, value = partial_of(packed_ref, weight_ref, pair)
        value = jnp.concatenate([value.astype(bf16), ones], axis=1)
        sums += jnp.dot(one_hot, value, preferred_element_type=f32)
    values = jnp.dot(rows_ref[...], dim_weight_ref[...], preferred_element_type=f32).astype(bf16)
    diagonal = diagonal_of(ring_keys, out_width)
    own = pl.ds(0, ring_keys)
    for m in range(members):
        part = sums[m * ring_keys : (m + 1) * ring_keys]
        out_ref[m, own, pl.ds(0, out_width)] = part[:, :out_width].astype(bf16)
        out_ref[m, own, pl.ds(out_width, out_width)] = values
        counts = jnp.where(diagonal, part[:, out_width:], f32(0.0)).sum(axis=0, keepdims=True)
        high = jnp.floor(counts * (1.0 / digit))
        digits = jnp.concatenate([high, counts - high * digit], axis=1)
        digits = jnp.broadcast_to(digits, (extra_rows, two_widths))
        out_ref[m, pl.ds(ring_keys, extra_rows), :] = digits.astype(bf16)


def both_terms(packed_ref, weight_ref, rows_ref, met_ref, kept_ref, given_ref):
    members, _, two_widths = met_ref.shape
    out_width = two_widths // 2
    ring_keys = rows_ref.shape[0]
    buckets = packed_ref.shape[0]
    bucket_rows = packed_ref.shape[1] - extra_rows
    width = weight_ref.shape[0]
    contract = (((0,), (0,)), ((), ()))

    own = pl.ds(0, ring_keys)
    values = jnp.concatenate(
        [met_ref[m, own, pl.ds(out_width, out_width)] for m in range(members)], axis=0
    )
    codes = jnp.concatenate([codes_of(packed_ref, b) for b in range(buckets)], axis=0)
    codes = jnp.transpose(codes.astype(f32)).astype(i32)
    places = lax.broadcasted_iota(i32, (bucket_rows, members * ring_keys), 1).astype(i16)
    fact_term = jnp.zeros((width, out_width), f32)
    for pair in pairs_of(packed_ref):
        one_hot = []
        for b in pair:
            code = jnp.broadcast_to(codes[:, b : b + 1], (bucket_rows, 128)).astype(i16)
            code = jnp.concatenate([code] * (members * ring_keys // 128), axis=1)
            one_hot.append(jnp.where(places == code, bf16(1.0), bf16(0.0)))
        features, value = partial_of(packed_ref, weight_ref, pair)
        found = jnp.dot(jnp.concatenate(one_hot, axis=0), values, preferred_element_type=f32)
        live = jnp.concatenate([codes[:, b : b + 1] for b in pair], axis=0) >= 0
        residual = jnp.where(live, value + found, f32(0.0)).astype(bf16)
        fact_term += lax.dot_general(features, residual, contract, preferred_element_type=f32)
    me = lax.rem(lax.axis_index("fact"), ring_size)
    sums = jnp.zeros((ring_keys, out_width), f32)
    digits = jnp.zeros((extra_rows, two_widths), f32)
    for m in range(members):
        sums += met_ref[m, own, pl.ds(0, out_width)].astype(f32)
        digits += met_ref[m, pl.ds(ring_keys, extra_rows), :].astype(f32)
    counts = digits[:1, :out_width] * digit + digits[:1, out_width:]
    diagonal = diagonal_of(ring_keys, out_width)
    counts = jnp.sum(jnp.where(diagonal, counts, f32(0.0)), axis=1, keepdims=True)
    sums += counts * met_ref[me, own, pl.ds(out_width, out_width)].astype(f32)
    high = sums.astype(bf16)
    low = (sums - high.astype(f32)).astype(bf16)
    dim_term = lax.dot_general(
        rows_ref[...], jnp.concatenate([high, low], axis=1), contract, preferred_element_type=f32
    )
    dim_term = dim_term[:, :out_width] + dim_term[:, out_width:]
    half = kept_ref.shape[0]

    def store(upper_ref, lower_ref):
        upper_ref[pl.ds(0, width), :] = fact_term
        upper_ref[pl.ds(width, half - width), :] = dim_term[: half - width]
        lower_ref[...] = dim_term[half - width :]

    core = lax.rem(lax.axis_index("key"), 2)
    pl.when(core == 0)(lambda: store(kept_ref, given_ref))
    pl.when(core == 1)(lambda: store(given_ref, kept_ref))


def finish(row_scale, totals_ref, fact_weight_ref, dim_weight_ref, fact_ref, dim_ref):
    width = fact_ref.shape[0]
    fact_ref[...] = totals_ref[pl.ds(0, width), :] * row_scale + ridge_weight * fact_weight_ref[
        ...
    ].astype(f32)
    dim_ref[...] = totals_ref[
        pl.ds(width, dim_ref.shape[0]), :
    ] * row_scale + ridge_weight * dim_weight_ref[...].astype(f32)


def kernel_call(body, shapes, dtype, *operands):
    vmem = pl.BlockSpec(memory_space=pltpu.VMEM)
    return pl.pallas_call(
        body,
        out_shape=tuple(jax.ShapeDtypeStruct(shape, dtype) for shape in shapes),
        in_specs=[vmem] * len(operands),
        out_specs=(vmem,) * len(shapes),
        compiler_params=pltpu.CompilerParams(vmem_limit_bytes=32 << 20),
    )(*operands)


def on_device(
    fact_features, targets, fact_keys, fill_counts, dim_features, fact_weight, dim_weight
):
    key_devices = lax.axis_size("key")
    fact_devices = lax.axis_size("fact")
    one_z, one_y, chip, plane = groups_of(fact_devices, key_devices)
    slot_count = fact_keys.shape[0]
    bucket_rows = slot_count // key_devices
    own_keys, dim_width = dim_features.shape
    fact_width, out_width = fact_weight.shape
    ring_keys = len(one_z) * own_keys

    packed = pl.pallas_call(
        functools.partial(pack_slots, own_keys, ring_keys),
        out_shape=jax.ShapeDtypeStruct(
            (key_devices, bucket_rows + extra_rows, fact_width + out_width), bf16
        ),
        in_specs=[pl.BlockSpec(memory_space=pl.ANY)] * 4,
        out_specs=pl.BlockSpec(memory_space=pl.ANY),
        scratch_shapes=[
            pltpu.VMEM((key_devices, bucket_rows), i32),
            pltpu.SMEM((1, key_devices), i32),
            pltpu.VMEM((key_devices, bucket_rows + extra_rows, fact_width + out_width), bf16),
            pltpu.SemaphoreType.DMA((key_devices // 2 + 1, 3)),
        ],
    )(
        fact_keys.reshape(key_devices, bucket_rows),
        fill_counts,
        fact_features.reshape(key_devices, bucket_rows, fact_width),
        targets.reshape(key_devices, bucket_rows, out_width),
    )
    packed = spread(packed, "key")
    rows = lax.all_gather(dim_features, "fact", axis=0, tiled=True, axis_index_groups=one_y)

    (met,) = kernel_call(
        sum_by_key,
        ((ring_size, ring_keys + extra_rows, 2 * out_width),),
        bf16,
        packed,
        fact_weight,
        rows,
        dim_weight,
    )
    met = spread(met, "fact", one_z)
    half = ((fact_width + dim_width) // 2, out_width)
    kept, given = kernel_call(both_terms, (half, half), f32, packed, fact_weight, rows, met)
    totals = total_over_devices(kept, given, one_y, chip, plane)
    total_rows = slot_count * fact_devices * key_devices
    row_scale = float(total_rows) ** (-0.5)
    vmem = pl.BlockSpec(memory_space=pltpu.VMEM)
    return tuple(
        pl.pallas_call(
            functools.partial(finish, row_scale),
            out_shape=(
                jax.ShapeDtypeStruct((fact_width, out_width), f32),
                jax.ShapeDtypeStruct((dim_width, out_width), f32),
            ),
            in_specs=[vmem] * 3,
            out_specs=(vmem, vmem),
            compiler_params=pltpu.CompilerParams(vmem_limit_bytes=16 << 20),
        )(totals, fact_weight, dim_weight)
    )


def solution(mesh):
    placed = (
        P(("fact", "key"), None),
        P(("fact", "key"), None),
        P(("fact", "key")),
        P(("fact", "key"), None),
        P(("fact", "key"), None),
        P(),
        P(),
    )
    return jax.shard_map(
        on_device, mesh=mesh, in_specs=placed, out_specs=(P(), P()), check_vma=False
    )
```

```python
import functools

import jax
import jax.numpy as jnp
from jax import lax
from jax.experimental import pallas as pl
from jax.experimental.pallas import tpu as pltpu
from jax.sharding import PartitionSpec as P

ridge_weight = 4.0
ring_size = 8
digit = 64
extra_rows = 8
f32, bf16, i32 = jnp.float32, jnp.bfloat16, jnp.int32


def groups_of(fact_devices, key_devices):
    levels = range(fact_devices // ring_size)
    chips, cores = range(key_devices // 2), range(2)
    one_z = [[z * ring_size + y for y in range(ring_size)] for z in levels]
    one_y = [[z * ring_size + y for z in levels] for y in range(ring_size)]
    near = [line[i : i + 4] for line in one_y for i in range(0, len(line), 4)]
    far = [line[i::4] for line in one_y for i in range(4)]
    chip = [[2 * x + core for core in cores] for x in chips]
    plane = [
        [(z * ring_size + y) * key_devices + 2 * x + core for y in range(ring_size) for x in chips]
        for z in levels
        for core in cores
    ]
    return one_z, one_y, near, far, chip, plane


def spread(array, axis, groups=None):
    return lax.all_to_all(
        array, axis, split_axis=0, concat_axis=0, tiled=True, axis_index_groups=groups
    )


def collect(array, axis, copies, groups):
    return spread(jnp.broadcast_to(array[None], (copies, *array.shape)), axis, groups)


def total_over_devices(kept, given, one_y, chip, plane):
    rows, width = kept.shape
    both = ("fact", "key")
    members = len(plane[0])
    swap = [(a, b) for pair in chip for a, b in (pair, pair[::-1])]
    part = kept + lax.ppermute(given, "key", swap)
    part = spread(part.reshape(members, -1, 4, width), both, plane).sum(axis=0)
    part = collect(part, "fact", len(one_y[0]), one_y).sum(axis=0)
    part = collect(part, both, members, plane).reshape(-1, 4, width)
    part = lax.all_gather(part, "key", axis=0, tiled=True, axis_index_groups=chip)
    return part.reshape(2 * rows, width)


def pack_slots(
    own_keys, ring_keys, keys_hbm, fill_hbm, features_hbm, targets_hbm, out_hbm, keys_ref, fill_ref, slots_ref, done
):
    buckets, bucket_rows, width = features_hbm.shape
    out_width = targets_hbm.shape[2]
    slots = pl.ds(0, bucket_rows)
    groups = range(buckets // 2)

    def copies(g):
        two = pl.ds(2 * g, 2)
        return (
            pltpu.make_async_copy(
                features_hbm.at[two], slots_ref.at[two, slots, pl.ds(0, width)], done.at[g, 0]
            ),
            pltpu.make_async_copy(
                targets_hbm.at[two], slots_ref.at[two, slots, pl.ds(width, out_width)], done.at[g, 1]
            ),
            pltpu.make_async_copy(slots_ref.at[two], out_hbm.at[two], done.at[g, 2]),
        )

    keys_in = pltpu.make_async_copy(keys_hbm, keys_ref, done.at[len(groups), 0])
    fill_in = pltpu.make_async_copy(fill_hbm, fill_ref, done.at[len(groups), 1])
    keys_in.start()
    fill_in.start()
    plan = [copies(g) for g in groups]
    for features_in, targets_in, _ in plan:
        features_in.start()
        targets_in.start()
    keys_in.wait()
    fill_in.wait()
    keys = keys_ref[...]
    owner = keys // (own_keys * buckets)
    places = (owner % ring_size) * ring_keys + (owner // ring_size) * own_keys + keys % own_keys
    slot = lax.broadcasted_iota(i32, (1, bucket_rows), 1)
    for b in range(buckets):
        codes = jnp.where(slot < fill_ref[0, b], places[b : b + 1], -digit)
        high = codes // digit
        low = codes - high * digit
        digits = jnp.concatenate([high, low, jnp.zeros_like(high)], axis=1).astype(f32)
        digits = jnp.broadcast_to(digits, (extra_rows, width + out_width))
        slots_ref[b, pl.ds(bucket_rows, extra_rows), :] = digits.astype(bf16)
    for features_in, targets_in, out in plan:
        features_in.wait()
        targets_in.wait()
        out.start()
    for _, _, out in plan:
        out.wait()


def codes_of(packed_ref, b):
    bucket_rows = packed_ref.shape[1] - extra_rows
    digits = packed_ref[b, pl.ds(bucket_rows, extra_rows), :].astype(f32)
    codes = digits[:, :bucket_rows] * digit + digits[:, bucket_rows : 2 * bucket_rows]
    return codes.astype(i32)[:1]


def partial_of(packed_ref, weight_ref, pair):
    slots = pl.ds(0, packed_ref.shape[1] - extra_rows)
    width = weight_ref.shape[0]
    rows = jnp.concatenate([packed_ref[b, slots, :] for b in pair], axis=0)
    features = rows[:, :width]
    value = jnp.dot(features, weight_ref[...], preferred_element_type=f32)
    return features, value - rows[:, width:].astype(f32)


def pairs_of(packed_ref):
    return [(b, b + 1) for b in range(0, packed_ref.shape[0], 2)]


def diagonal_of(rows, columns):
    return lax.broadcasted_iota(i32, (rows, columns), 0) == lax.broadcasted_iota(
        i32, (rows, columns), 1
    )


def split(value):
    high = value.astype(bf16)
    return high, (value - high.astype(f32)).astype(bf16)


contract = (((0,), (0,)), ((), ()))


def own_term(packed_ref, weight_ref, out_ref):
    out_width = weight_ref.shape[1]
    codes = [codes_of(packed_ref, b) for b in range(packed_ref.shape[0])]
    codes = jnp.transpose(jnp.concatenate(codes, axis=0).astype(f32))
    total = jnp.zeros((weight_ref.shape[0], 2 * out_width), f32)
    for pair in pairs_of(packed_ref):
        features, value = partial_of(packed_ref, weight_ref, pair)
        live = jnp.concatenate([codes[:, b : b + 1] for b in pair], axis=0) >= 0.0
        value = jnp.concatenate(split(jnp.where(live, value, f32(0.0))), axis=1)
        total += lax.dot_general(features, value, contract, preferred_element_type=f32)
    out_ref[...] = total[:, :out_width] + total[:, out_width:]


def sum_by_key(packed_ref, rows_ref, out_ref, rows_out_ref):
    members, _, width = out_ref.shape
    ring_keys = out_ref.shape[1] - extra_rows
    bucket_rows = packed_ref.shape[1] - extra_rows
    slots = pl.ds(0, bucket_rows)
    places = lax.broadcasted_iota(i32, (members * ring_keys, 2 * bucket_rows), 0)
    ones = jnp.ones((2 * bucket_rows, 128), bf16)
    sums = jnp.zeros((members * ring_keys, width + 128), f32)
    for pair in pairs_of(packed_ref):
        codes = jnp.concatenate([codes_of(packed_ref, b) for b in pair], axis=1)
        one_hot = jnp.where(places == codes, f32(1.0), f32(0.0)).astype(bf16)
        value = jnp.concatenate([packed_ref[b, slots, :] for b in pair], axis=0)
        value = jnp.concatenate([value, ones], axis=1)
        sums += jnp.dot(one_hot, value, preferred_element_type=f32)
    diagonal = diagonal_of(ring_keys, 128)
    for m in range(members):
        part = sums[m * ring_keys : (m + 1) * ring_keys]
        out_ref[m, pl.ds(0, ring_keys), :] = part[:, :width].astype(bf16)
        counts = jnp.where(diagonal, part[:, width:], f32(0.0)).sum(axis=0, keepdims=True)
        high = jnp.floor(counts * (1.0 / digit))
        rest = jnp.zeros((1, width - 256), f32)
        digits = jnp.concatenate([high, counts - high * digit, rest], axis=1)
        out_ref[m, pl.ds(ring_keys, extra_rows), :] = jnp.broadcast_to(
            digits, (extra_rows, width)
        ).astype(bf16)
    rows_out_ref[...] = rows_ref[...]


def both_terms(own_ref, weight_ref, rows_ref, dim_weight_ref, met_ref, kept_ref, given_ref):
    members = met_ref.shape[0]
    ring_keys, dim_width = rows_ref.shape
    width, out_width = weight_ref.shape
    keys = pl.ds(0, ring_keys)
    rows = rows_ref[...]
    values = jnp.dot(rows, dim_weight_ref[...], preferred_element_type=f32).astype(bf16)
    met = jnp.zeros((ring_keys, width + out_width), f32)
    digits = jnp.zeros((extra_rows, width + out_width), f32)
    for m in range(members):
        met += met_ref[m, keys, :].astype(f32)
        digits += met_ref[m, pl.ds(ring_keys, extra_rows), :].astype(f32)
    counts = digits[:1, :128] * digit + digits[:1, 128:256]
    diagonal = diagonal_of(ring_keys, 128)
    counts = jnp.sum(jnp.where(diagonal, counts, f32(0.0)), axis=1, keepdims=True)
    high, low = split(met[:, :width])
    sums = jnp.dot(high, weight_ref[...], preferred_element_type=f32)
    sums += jnp.dot(low, weight_ref[...], preferred_element_type=f32)
    sums += counts * values.astype(f32) - met[:, width:]
    fact_term = own_ref[...]
    fact_term += lax.dot_general(high, values, contract, preferred_element_type=f32)
    fact_term += lax.dot_general(low, values, contract, preferred_element_type=f32)
    sums = jnp.concatenate(split(sums), axis=1)
    dim_term = lax.dot_general(rows, sums, contract, preferred_element_type=f32)
    dim_term = dim_term[:, :out_width] + dim_term[:, out_width:]
    half = kept_ref.shape[0]

    def store(upper_ref, lower_ref):
        upper_ref[pl.ds(0, width), :] = fact_term
        upper_ref[pl.ds(width, half - width), :] = dim_term[: half - width]
        lower_ref[...] = dim_term[half - width :]

    core = lax.rem(lax.axis_index("key"), 2)
    pl.when(core == 0)(lambda: store(kept_ref, given_ref))
    pl.when(core == 1)(lambda: store(given_ref, kept_ref))


def finish(row_scale, totals_ref, fact_weight_ref, dim_weight_ref, fact_ref, dim_ref):
    width = fact_ref.shape[0]
    fact_ref[...] = totals_ref[pl.ds(0, width), :] * row_scale + ridge_weight * fact_weight_ref[
        ...
    ].astype(f32)
    dim_ref[...] = totals_ref[
        pl.ds(width, dim_ref.shape[0]), :
    ] * row_scale + ridge_weight * dim_weight_ref[...].astype(f32)


def kernel_call(body, outs, *operands):
    vmem = pl.BlockSpec(memory_space=pltpu.VMEM)
    return pl.pallas_call(
        body,
        out_shape=tuple(jax.ShapeDtypeStruct(shape, dtype) for shape, dtype in outs),
        in_specs=[vmem] * len(operands),
        out_specs=(vmem,) * len(outs),
        compiler_params=pltpu.CompilerParams(vmem_limit_bytes=32 << 20),
    )(*operands)


def on_device(
    fact_features, targets, fact_keys, fill_counts, dim_features, fact_weight, dim_weight
):
    key_devices = lax.axis_size("key")
    fact_devices = lax.axis_size("fact")
    one_z, one_y, near, far, chip, plane = groups_of(fact_devices, key_devices)
    slot_count = fact_keys.shape[0]
    bucket_rows = slot_count // key_devices
    own_keys, dim_width = dim_features.shape
    fact_width, out_width = fact_weight.shape
    ring_keys = len(one_z) * own_keys

    packed = pl.pallas_call(
        functools.partial(pack_slots, own_keys, ring_keys),
        out_shape=jax.ShapeDtypeStruct(
            (key_devices, bucket_rows + extra_rows, fact_width + out_width), bf16
        ),
        in_specs=[pl.BlockSpec(memory_space=pl.ANY)] * 4,
        out_specs=pl.BlockSpec(memory_space=pl.ANY),
        scratch_shapes=[
            pltpu.VMEM((key_devices, bucket_rows), i32),
            pltpu.SMEM((1, key_devices), i32),
            pltpu.VMEM((key_devices, bucket_rows + extra_rows, fact_width + out_width), bf16),
            pltpu.SemaphoreType.DMA((key_devices // 2 + 1, 3)),
        ],
    )(
        fact_keys.reshape(key_devices, bucket_rows),
        fill_counts,
        fact_features.reshape(key_devices, bucket_rows, fact_width),
        targets.reshape(key_devices, bucket_rows, out_width),
    )
    slots = spread(packed, "key")
    rows = lax.all_gather(dim_features, "fact", axis=0, tiled=True, axis_index_groups=near)
    (own,) = kernel_call(own_term, (((fact_width, out_width), f32),), packed, fact_weight)

    block = (ring_size, ring_keys + extra_rows, fact_width + out_width)
    met, rows = kernel_call(sum_by_key, ((block, bf16), (rows.shape, bf16)), slots, rows)
    met = spread(met, "fact", one_z)
    rows = lax.all_gather(rows, "fact", axis=0, tiled=True, axis_index_groups=far)
    half = (((fact_width + dim_width) // 2, out_width), f32)
    kept, given = kernel_call(both_terms, (half, half), own, fact_weight, rows, dim_weight, met)
    totals = total_over_devices(kept, given, one_y, chip, plane)
    total_rows = slot_count * fact_devices * key_devices
    row_scale = float(total_rows) ** (-0.5)
    vmem = pl.BlockSpec(memory_space=pltpu.VMEM)
    return tuple(
        pl.pallas_call(
            functools.partial(finish, row_scale),
            out_shape=(
                jax.ShapeDtypeStruct((fact_width, out_width), f32),
                jax.ShapeDtypeStruct((dim_width, out_width), f32),
            ),
            in_specs=[vmem] * 3,
            out_specs=(vmem, vmem),
            compiler_params=pltpu.CompilerParams(vmem_limit_bytes=16 << 20),
        )(totals, fact_weight, dim_weight)
    )


def solution(mesh):
    placed = (
        P(("fact", "key"), None),
        P(("fact", "key"), None),
        P(("fact", "key")),
        P(("fact", "key"), None),
        P(("fact", "key"), None),
        P(),
        P(),
    )
    return jax.shard_map(
        on_device, mesh=mesh, in_specs=placed, out_specs=(P(), P()), check_vma=False
    )
```

```python
import functools

import jax
import jax.numpy as jnp
from jax import lax
from jax.experimental import pallas as pl
from jax.experimental.pallas import tpu as pltpu
from jax.sharding import PartitionSpec as P

ridge_weight = 4.0
ring_size = 8
digit = 64
extra_rows = 16
f32, bf16, i32 = jnp.float32, jnp.bfloat16, jnp.int32


def groups_of(fact_devices, key_devices):
    levels = range(fact_devices // ring_size)
    chips, cores = range(key_devices // 2), range(2)
    one_z = [[z * ring_size + y for y in range(ring_size)] for z in levels]
    one_y = [[z * ring_size + y for z in levels] for y in range(ring_size)]
    chip = [[2 * x + core for core in cores] for x in chips]
    plane = [
        [(z * ring_size + y) * key_devices + 2 * x + core for y in range(ring_size) for x in chips]
        for z in levels
        for core in cores
    ]
    return one_z, one_y, chip, plane


def spread(array, axis, groups=None):
    return lax.all_to_all(
        array, axis, split_axis=0, concat_axis=0, tiled=True, axis_index_groups=groups
    )


def collect(array, axis, copies, groups):
    return spread(jnp.broadcast_to(array[None], (copies, *array.shape)), axis, groups)


def total_over_devices(kept, given, one_y, chip, plane):
    rows, width = kept.shape
    both = ("fact", "key")
    members = len(plane[0])
    swap = [(a, b) for pair in chip for a, b in (pair, pair[::-1])]
    part = kept + lax.ppermute(given, "key", swap)
    part = spread(part.reshape(members, -1, 4, width), both, plane).sum(axis=0)
    part = collect(part, "fact", len(one_y[0]), one_y).sum(axis=0)
    part = collect(part, both, members, plane).reshape(-1, 4, width)
    part = lax.all_gather(part, "key", axis=0, tiled=True, axis_index_groups=chip)
    return part.reshape(2 * rows, width)


def pack_slots(
    own_keys, ring_keys, keys_hbm, fill_hbm, features_hbm, targets_hbm, out_hbm, keys_ref, fill_ref, slots_ref, done
):
    buckets, bucket_rows, width = features_hbm.shape
    out_width = targets_hbm.shape[2]
    slots = pl.ds(0, bucket_rows)
    groups = range(buckets // 2)

    def copies(g):
        two = pl.ds(2 * g, 2)
        return (
            pltpu.make_async_copy(
                features_hbm.at[two], slots_ref.at[two, slots, pl.ds(0, width)], done.at[g, 0]
            ),
            pltpu.make_async_copy(
                targets_hbm.at[two], slots_ref.at[two, slots, pl.ds(width, out_width)], done.at[g, 1]
            ),
            pltpu.make_async_copy(slots_ref.at[two], out_hbm.at[two], done.at[g, 2]),
        )

    keys_in = pltpu.make_async_copy(keys_hbm, keys_ref, done.at[len(groups), 0])
    fill_in = pltpu.make_async_copy(fill_hbm, fill_ref, done.at[len(groups), 1])
    keys_in.start()
    fill_in.start()
    for g in groups:
        for copy in copies(g)[:2]:
            copy.start()
    keys_in.wait()
    fill_in.wait()
    keys = keys_ref[...]
    owner = keys // (own_keys * buckets)
    places = (owner % ring_size) * ring_keys + (owner // ring_size) * own_keys + keys % own_keys
    slot = lax.broadcasted_iota(i32, (1, bucket_rows), 1)
    for b in range(buckets):
        codes = jnp.where(slot < fill_ref[0, b], places[b : b + 1], -digit)
        high = codes // digit
        low = codes - high * digit
        digits = jnp.concatenate([high, low, jnp.zeros_like(high)], axis=1).astype(f32)
        digits = jnp.broadcast_to(digits, (extra_rows, width + out_width))
        slots_ref[b, pl.ds(bucket_rows, extra_rows), :] = digits.astype(bf16)
    for g in groups:
        features_in, targets_in, out = copies(g)
        features_in.wait()
        targets_in.wait()
        out.start()
    for g in groups:
        copies(g)[2].wait()


def codes_of(packed_ref, b):
    bucket_rows = packed_ref.shape[1] - extra_rows
    digits = packed_ref[b, pl.ds(bucket_rows, extra_rows), :].astype(f32)
    codes = digits[:, :bucket_rows] * digit + digits[:, bucket_rows : 2 * bucket_rows]
    return codes.astype(i32)[:1]


def partial_of(packed_ref, weight_ref, pair):
    slots = pl.ds(0, packed_ref.shape[1] - extra_rows)
    width = weight_ref.shape[0]
    rows = jnp.concatenate([packed_ref[b, slots, :] for b in pair], axis=0)
    features = rows[:, :width]
    value = jnp.dot(features, weight_ref[...], preferred_element_type=f32)
    return features, value - rows[:, width:].astype(f32)


def pairs_of(packed_ref):
    return [(b, b + 1) for b in range(0, packed_ref.shape[0], 2)]


def diagonal_of(rows, columns):
    return lax.broadcasted_iota(i32, (rows, columns), 0) == lax.broadcasted_iota(
        i32, (rows, columns), 1
    )


def sum_by_key(packed_ref, weight_ref, rows_ref, dim_weight_ref, out_ref):
    members, _, two_widths = out_ref.shape
    out_width = two_widths // 2
    ring_keys = rows_ref.shape[0]
    two_rows = 2 * (packed_ref.shape[1] - extra_rows)
    places = lax.broadcasted_iota(i32, (members * ring_keys, two_rows), 0)
    ones = jnp.ones((two_rows, out_width), bf16)
    sums = jnp.zeros((members * ring_keys, two_widths), f32)
    for pair in pairs_of(packed_ref):
        codes = jnp.concatenate([codes_of(packed_ref, b) for b in pair], axis=1)
        one_hot = jnp.where(places == codes, f32(1.0), f32(0.0)).astype(bf16)
        _, value = partial_of(packed_ref, weight_ref, pair)
        value = jnp.concatenate([value.astype(bf16), ones], axis=1)
        sums += jnp.dot(one_hot, value, preferred_element_type=f32)
    values = jnp.dot(rows_ref[...], dim_weight_ref[...], preferred_element_type=f32).astype(bf16)
    diagonal = diagonal_of(ring_keys, out_width)
    own = pl.ds(0, ring_keys)
    for m in range(members):
        part = sums[m * ring_keys : (m + 1) * ring_keys]
        out_ref[m, own, pl.ds(0, out_width)] = part[:, :out_width].astype(bf16)
        out_ref[m, own, pl.ds(out_width, out_width)] = values
        counts = jnp.where(diagonal, part[:, out_width:], f32(0.0)).sum(axis=0, keepdims=True)
        high = jnp.floor(counts * (1.0 / digit))
        digits = jnp.concatenate([high, counts - high * digit], axis=1)
        digits = jnp.broadcast_to(digits, (extra_rows, two_widths))
        out_ref[m, pl.ds(ring_keys, extra_rows), :] = digits.astype(bf16)


def both_terms(packed_ref, weight_ref, rows_ref, met_ref, kept_ref, given_ref):
    members, _, two_widths = met_ref.shape
    out_width = two_widths // 2
    ring_keys = rows_ref.shape[0]
    buckets = packed_ref.shape[0]
    bucket_rows = packed_ref.shape[1] - extra_rows
    width = weight_ref.shape[0]
    contract = (((0,), (0,)), ((), ()))

    own = pl.ds(0, ring_keys)
    values = jnp.concatenate(
        [met_ref[m, own, pl.ds(out_width, out_width)] for m in range(members)], axis=0
    )
    codes = jnp.concatenate([codes_of(packed_ref, b) for b in range(buckets)], axis=0)
    codes = jnp.transpose(codes.astype(f32)).astype(i32)
    places = lax.broadcasted_iota(i32, (bucket_rows, members * ring_keys), 1)
    fact_term = jnp.zeros((width, out_width), f32)
    for pair in pairs_of(packed_ref):
        one_hot = [
            jnp.where(places == codes[:, b : b + 1], f32(1.0), f32(0.0)).astype(bf16) for b in pair
        ]
        features, value = partial_of(packed_ref, weight_ref, pair)
        found = jnp.dot(jnp.concatenate(one_hot, axis=0), values, preferred_element_type=f32)
        live = jnp.concatenate([codes[:, b : b + 1] for b in pair], axis=0) >= 0
        residual = jnp.where(live, value + found, f32(0.0)).astype(bf16)
        fact_term += lax.dot_general(features, residual, contract, preferred_element_type=f32)
    me = lax.rem(lax.axis_index("fact"), ring_size)
    sums = jnp.zeros((ring_keys, out_width), f32)
    digits = jnp.zeros((extra_rows, two_widths), f32)
    for m in range(members):
        sums += met_ref[m, own, pl.ds(0, out_width)].astype(f32)
        digits += met_ref[m, pl.ds(ring_keys, extra_rows), :].astype(f32)
    counts = digits[:1, :out_width] * digit + digits[:1, out_width:]
    diagonal = diagonal_of(ring_keys, out_width)
    counts = jnp.sum(jnp.where(diagonal, counts, f32(0.0)), axis=1, keepdims=True)
    sums += counts * met_ref[me, own, pl.ds(out_width, out_width)].astype(f32)
    high = sums.astype(bf16)
    low = (sums - high.astype(f32)).astype(bf16)
    dim_term = lax.dot_general(
        rows_ref[...], jnp.concatenate([high, low], axis=1), contract, preferred_element_type=f32
    )
    dim_term = dim_term[:, :out_width] + dim_term[:, out_width:]
    half = kept_ref.shape[0]

    def store(upper_ref, lower_ref):
        upper_ref[pl.ds(0, width), :] = fact_term
        upper_ref[pl.ds(width, half - width), :] = dim_term[: half - width]
        lower_ref[...] = dim_term[half - width :]

    core = lax.rem(lax.axis_index("key"), 2)
    pl.when(core == 0)(lambda: store(kept_ref, given_ref))
    pl.when(core == 1)(lambda: store(given_ref, kept_ref))


def finish(row_scale, totals_ref, fact_weight_ref, dim_weight_ref, fact_ref, dim_ref):
    width = fact_ref.shape[0]
    fact_ref[...] = totals_ref[pl.ds(0, width), :] * row_scale + ridge_weight * fact_weight_ref[
        ...
    ].astype(f32)
    dim_ref[...] = totals_ref[
        pl.ds(width, dim_ref.shape[0]), :
    ] * row_scale + ridge_weight * dim_weight_ref[...].astype(f32)


def kernel_call(body, shapes, dtype, *operands):
    vmem = pl.BlockSpec(memory_space=pltpu.VMEM)
    return pl.pallas_call(
        body,
        out_shape=tuple(jax.ShapeDtypeStruct(shape, dtype) for shape in shapes),
        in_specs=[vmem] * len(operands),
        out_specs=(vmem,) * len(shapes),
        compiler_params=pltpu.CompilerParams(vmem_limit_bytes=32 << 20),
    )(*operands)


def on_device(
    fact_features, targets, fact_keys, fill_counts, dim_features, fact_weight, dim_weight
):
    key_devices = lax.axis_size("key")
    fact_devices = lax.axis_size("fact")
    one_z, one_y, chip, plane = groups_of(fact_devices, key_devices)
    slot_count = fact_keys.shape[0]
    bucket_rows = slot_count // key_devices
    own_keys, dim_width = dim_features.shape
    fact_width, out_width = fact_weight.shape
    ring_keys = len(one_z) * own_keys

    packed = pl.pallas_call(
        functools.partial(pack_slots, own_keys, ring_keys),
        out_shape=jax.ShapeDtypeStruct(
            (key_devices, bucket_rows + extra_rows, fact_width + out_width), bf16
        ),
        in_specs=[pl.BlockSpec(memory_space=pl.ANY)] * 4,
        out_specs=pl.BlockSpec(memory_space=pl.ANY),
        scratch_shapes=[
            pltpu.VMEM((key_devices, bucket_rows), i32),
            pltpu.SMEM((1, key_devices), i32),
            pltpu.VMEM((key_devices, bucket_rows + extra_rows, fact_width + out_width), bf16),
            pltpu.SemaphoreType.DMA((key_devices // 2 + 1, 3)),
        ],
    )(
        fact_keys.reshape(key_devices, bucket_rows),
        fill_counts,
        fact_features.reshape(key_devices, bucket_rows, fact_width),
        targets.reshape(key_devices, bucket_rows, out_width),
    )
    packed = spread(packed, "key")
    rows = lax.all_gather(dim_features, "fact", axis=0, tiled=True, axis_index_groups=one_y)

    (met,) = kernel_call(
        sum_by_key,
        ((ring_size, ring_keys + extra_rows, 2 * out_width),),
        bf16,
        packed,
        fact_weight,
        rows,
        dim_weight,
    )
    met = spread(met, "fact", one_z)
    half = ((fact_width + dim_width) // 2, out_width)
    kept, given = kernel_call(both_terms, (half, half), f32, packed, fact_weight, rows, met)
    totals = total_over_devices(kept, given, one_y, chip, plane)
    total_rows = slot_count * fact_devices * key_devices
    row_scale = float(total_rows) ** (-0.5)
    vmem = pl.BlockSpec(memory_space=pltpu.VMEM)
    return tuple(
        pl.pallas_call(
            functools.partial(finish, row_scale),
            out_shape=(
                jax.ShapeDtypeStruct((fact_width, out_width), f32),
                jax.ShapeDtypeStruct((dim_width, out_width), f32),
            ),
            in_specs=[vmem] * 3,
            out_specs=(vmem, vmem),
            compiler_params=pltpu.CompilerParams(vmem_limit_bytes=16 << 20),
        )(totals, fact_weight, dim_weight)
    )


def solution(mesh):
    placed = (
        P(("fact", "key"), None),
        P(("fact", "key"), None),
        P(("fact", "key")),
        P(("fact", "key"), None),
        P(("fact", "key"), None),
        P(),
        P(),
    )
    return jax.shard_map(
        on_device, mesh=mesh, in_specs=placed, out_specs=(P(), P()), check_vma=False
    )
```
